128 devices in a mesh: month: 8 (over y, core), cols: 16 (over x, z).
Axes of the slice: x: 4, y: 4, z: 4, core: 2. Of those that a mesh axis runs over, the one named last changes fastest.
Arguments:
- forcing: float32 [8, 256, 6, 128], P('month', 'cols'), may hold values from -6 to 6
- tiles: bfloat16 [8, 4096, 128, 128], P('month', 'cols'), may hold values from -0.21875 to 0.21875
- tile_rows: int32 [8, 4096], P('month', 'cols'), may hold values from 0 to 255, as said below
- tile_cols: int32 [8, 4096], P('month', 'cols'), may hold values from 0 to 255, as said below
- tile_count: int32 [8, 16], P('month', 'cols'), may hold values from 1 to 256, as said below
- depth: int32 [256, 16], P('cols'), may hold values from 1 to 8
Outputs:
- adjoint: float32 [8, 256, 6, 128], P('month', 'cols')
The draws below stay inside these ranges and needn't reach their ends.
Inputs may be any that keep to these rules, and one draw needn't show every extreme that they name: `tile_cols`: the tiles held by cols index c take their column blocks from c's own blocks, c * 16 to (c + 1) * 16 - 1. `tile_rows`: the tiles held by cols index c take their row blocks from the blocks of c, of its two neighbours c - 1 and c + 1, and of the index c + 8, all counted modulo 256 / 16. `tile_count`: in each month one cols index has all 256 slots live; slots from the count on are unused.
All inputs are finite; a program needn't handle non-finite values.
Results may differ from the reference program's by a relative error of at most 0.022.
Values may be sent and summed in bfloat16 or wider, within the bound.
A program may use at most 64 MiB of HBM per device.

```python
import jax
import jax.numpy as jnp

BLOCK = 128
LEVELS = 8
TRACERS = 6
BLK_DEV = 16
TILE_DEV = 256
MONTHS = 8
NBLK = 256


def draw_tile_rows(key, part):
    slots = NBLK * TILE_DEV // BLK_DEV
    owners = NBLK // BLK_DEV
    slot = jnp.arange(slots, dtype=jnp.int32)
    owner = slot // TILE_DEV
    side = jax.random.randint(jax.random.fold_in(key, 11), (MONTHS, slots), 0, 4, dtype=jnp.int32)
    side = jnp.where((slot % TILE_DEV == 0)[None, :], 3, side)
    delta = jnp.where(side == 1, -1, jnp.where(side == 2, 1, jnp.where(side == 3, owners // 2, 0))).astype(jnp.int32)
    target = (owner[None, :] + delta + owners) % owners
    offset = jax.random.randint(jax.random.fold_in(key, 13), (MONTHS, slots), 0, BLK_DEV, dtype=jnp.int32)
    return (target * BLK_DEV + offset).astype(jnp.int32)


def draw_tile_cols(key, part):
    slots = NBLK * TILE_DEV // BLK_DEV
    owner = jnp.arange(slots, dtype=jnp.int32) // TILE_DEV
    offset = jax.random.randint(jax.random.fold_in(key, 17), (MONTHS, slots), 0, BLK_DEV, dtype=jnp.int32)
    return (owner[None, :] * BLK_DEV + offset).astype(jnp.int32)


def draw_tile_count(key, part):
    owners = NBLK // BLK_DEV
    base = jax.random.randint(jax.random.fold_in(key, 3), (MONTHS, owners), 1, TILE_DEV // 2 + 1, dtype=jnp.int32)
    pick = jax.random.randint(jax.random.fold_in(key, 5), (MONTHS, 1), 0, owners, dtype=jnp.int32)
    where_top = jnp.arange(owners, dtype=jnp.int32)[None, :] == pick
    return jnp.where(where_top, TILE_DEV, base).astype(jnp.int32)


def place_ends(result, own_key, low, high):
    longest = result.shape.index(max(result.shape))
    spots = []
    for shift in (0, 1):
        where = [jax.random.randint(jax.random.fold_in(own_key, axis), (), 0, length) for axis, length in enumerate(result.shape)]
        where[longest] = (where[longest] + shift) % result.shape[longest]
        spots.append(tuple(where))
    return result.at[spots[0]].set(low).at[spots[1]].set(high)


def block_scale(rng, extent, cuts, least, largest):
    level = 1.0
    for position, blocks in cuts:
        draws = jax.random.uniform(jax.random.fold_in(jax.random.fold_in(rng, 6), position), (blocks,), jnp.float32, least / len(cuts), largest / len(cuts))
        level = level * jnp.repeat(jnp.exp(draws), extent[position] // blocks).reshape((-1,) + (1,) * (len(extent) - 1 - position))
    return level


def scatter_about(own_key, extent, deviation, most, shards=(), held_as=jnp.bfloat16):
    loudness = block_scale(own_key, extent, shards, -0.22, 0.18) if shards else 1.0
    entries = jax.random.normal(own_key, extent, jnp.float32) * deviation * loudness
    return jnp.minimum(jnp.maximum(entries, -most), most).astype(held_as)


def setup_inputs(seed: int = 0) -> dict:
    splits = jax.random.split(jax.random.key(seed), 7)
    return {
        "forcing": scatter_about(splits[0], (MONTHS, NBLK, TRACERS, BLOCK), 1.0, 6.0, ((0, 8), (1, 16)), jnp.float32),
        "tiles": scatter_about(splits[1], (MONTHS, NBLK * TILE_DEV // BLK_DEV, BLOCK, BLOCK), (BLOCK * TILE_DEV // (3 * BLK_DEV)) ** -0.5, 0.21875, ((0, 8), (1, 16))),
        "tile_rows": draw_tile_rows(jax.random.fold_in(splits[6], 71), 0),
        "tile_cols": draw_tile_cols(jax.random.fold_in(splits[6], 71), 0),
        "tile_count": draw_tile_count(jax.random.fold_in(splits[6], 71), 0),
        "depth": place_ends(jax.random.randint(splits[5], (NBLK, BLOCK // LEVELS), 1, LEVELS + 1), jax.random.fold_in(splits[5], 1), 1, LEVELS).astype(jnp.int32),
    }


def wet_mask(depth):
    width = depth.shape[1]
    level = jnp.arange(BLOCK, dtype=jnp.int32) // width
    spread = jnp.tile(depth, (1, LEVELS))
    return (level[None, :] < spread).astype(jnp.float32)[:, None, :]


def month_step(state, forcing_m, tiles_m, rows_m, cols_m, count_m, wet):
    x_vals = (state + forcing_m).astype(jnp.bfloat16)
    picked = x_vals[cols_m].astype(jnp.float32)
    terms = jnp.einsum("stj,sij->sti", picked, tiles_m.astype(jnp.float32))
    slot = jnp.arange(rows_m.shape[0], dtype=jnp.int32)
    live = ((slot % TILE_DEV) < count_m[slot // TILE_DEV]).astype(jnp.float32)
    terms = terms * live[:, None, None]
    summed = jnp.zeros(state.shape, jnp.float32).at[rows_m].add(terms)
    return wet * summed


def reference(forcing, tiles, tile_rows, tile_cols, tile_count, depth):
    wet = wet_mask(depth)
    state = jnp.zeros(forcing.shape[1:], jnp.float32)
    results = [None] * MONTHS
    for sweep in range(2):
        for month in range(MONTHS - 1, -1, -1):
            state = month_step(state, forcing[month], tiles[month], tile_rows[month], tile_cols[month], tile_count[month], wet)
            if sweep == 1:
                results[month] = state
    return jnp.stack(results)
```

```python
import functools

import jax
import jax.numpy as jnp
from jax import lax
from jax.experimental import pallas as pl
from jax.experimental.pallas import tpu as pltpu
from jax.sharding import PartitionSpec as P

MESH = pl.DeviceIdType.MESH
CHUNKS = 8


def kernel(
    dims,
    cols_ref,
    count_ref,
    rows_ref,
    depth_ref,
    forcing_ref,
    tiles_ref,
    out_ref,
    tiles_v,
    x_rows,
    terms,
    pick,
    back_v,
    wet_v,
    send_v,
    recv_v,
    tile_sem,
    send_sem,
    recv_sem,
    back_send,
    back_recv,
):
    months, ncols, blk, tracers, block, slots, levels = dims
    deltas = (0, ncols - 1, 1, ncols // 2)
    ngroups = len(deltas)
    pad = x_rows.shape[1]
    per_chunk = slots // CHUNKS
    month = lax.axis_index("month")
    here = lax.axis_index("cols")
    earlier = lax.rem(month + months - 1, months)
    later = lax.rem(month + 1, months)
    last = months - 1

    def tile_copy(k):
        part = pl.ds(k * per_chunk, per_chunk)
        return pltpu.make_async_copy(tiles_ref.at[part], tiles_v.at[part], tile_sem.at[k])

    for k in range(CHUNKS):
        tile_copy(k).start()

    barrier = pltpu.get_barrier_semaphore()
    for other in (earlier, later):
        for delta in deltas:
            pl.semaphore_signal(
                barrier, inc=1,
                device_id={"month": other, "cols": lax.rem(here + delta, ncols)},
                device_id_type=MESH,
            )

    @pl.when(month == 0)
    def _():
        for delta in deltas[1:]:
            pl.semaphore_signal(
                barrier, inc=1,
                device_id={"month": month, "cols": lax.rem(here + delta, ncols)},
                device_id_type=MESH,
            )

    spread = (
        lax.broadcasted_iota(jnp.int32, (depth_ref.shape[1], block), 1) % depth_ref.shape[1]
        == lax.broadcasted_iota(jnp.int32, (depth_ref.shape[1], block), 0)
    ).astype(jnp.float32).astype(jnp.bfloat16)
    deep = jnp.dot(
        depth_ref[...].astype(jnp.float32).astype(jnp.bfloat16), spread,
        preferred_element_type=jnp.float32,
    )
    level = (lax.broadcasted_iota(jnp.int32, (blk, block), 1) // depth_ref.shape[1]).astype(jnp.float32)
    wet_v[...] = (level < deep).astype(jnp.float32)
    x_rows[...] = jnp.zeros_like(x_rows)
    live = lax.broadcasted_iota(jnp.int32, (blk, slots), 1) < count_ref[0, 0]
    inside = lax.broadcasted_iota(jnp.int32, (blk, slots), 0)
    for g, delta in enumerate(deltas):
        target = lax.rem(here + delta, ncols) * blk
        hit = ((inside + target) == rows_ref[...]) & live
        pick[g * blk:(g + 1) * blk, :] = hit.astype(jnp.float32).astype(jnp.bfloat16)

    def meet():
        @pl.when(month == 0)
        def _():
            pl.semaphore_wait(barrier, 3 * ngroups - 1)

        @pl.when(month != 0)
        def _():
            pl.semaphore_wait(barrier, 2 * ngroups)

    def set_x(x):
        x = x.astype(jnp.bfloat16).astype(jnp.float32)
        for t in range(tracers):
            x_rows[:, t, :] = x[t]

    def pair(g, swapped):
        s = 2 * g
        zero = jnp.zeros((pad, block), jnp.float32)
        xa = x_rows[cols_ref[0, s] & (blk - 1)]
        xb = x_rows[cols_ref[0, s + 1] & (blk - 1)]
        lhs = jnp.concatenate(
            [
                jnp.concatenate([xa, zero], 0).astype(jnp.bfloat16),
                jnp.concatenate([zero, xb], 0).astype(jnp.bfloat16),
            ], 1,
        )
        two = tiles_v[pl.ds(s, 2)]
        if swapped:
            out = jnp.dot(lhs, two.reshape(2 * block, block), preferred_element_type=jnp.float32)
        else:
            out = lax.dot_general(
                lhs, jnp.concatenate([two[0], two[1]], 1), (((1,), (1,)), ((), ())),
                preferred_element_type=jnp.float32,
            )
        terms[pl.ds(s * pad, 2 * pad), :] = out

    def link(sweep, g, target_month):
        slot = sweep + (month == 0).astype(jnp.int32)
        return pltpu.make_async_remote_copy(
            src_ref=send_v.at[sweep, g],
            dst_ref=recv_v.at[slot, g],
            send_sem=send_sem.at[sweep, g],
            recv_sem=recv_sem.at[slot, g],
            device_id={"month": target_month, "cols": lax.rem(here + deltas[g], ncols)},
            device_id_type=MESH,
        )

    def arrival(slot, g):
        return pltpu.make_async_remote_copy(
            src_ref=send_v.at[0, g],
            dst_ref=recv_v.at[slot, g],
            send_sem=send_sem.at[0, g],
            recv_sem=recv_sem.at[slot, g],
            device_id={"month": earlier, "cols": here},
            device_id_type=MESH,
        )

    def back(target_month):
        return pltpu.make_async_remote_copy(
            src_ref=back_v,
            dst_ref=out_ref,
            send_sem=back_send,
            recv_sem=back_recv,
            device_id={"month": target_month, "cols": here},
            device_id_type=MESH,
        )

    def gather_rows(sweep):
        for t in range(tracers):
            terms_t = terms[pl.ds(t, slots, stride=pad), :].astype(jnp.bfloat16)
            part = jnp.dot(pick[...], terms_t, preferred_element_type=jnp.float32)
            part = part.astype(jnp.bfloat16)
            for g in range(ngroups):
                send_v[sweep, g, t] = part[g * blk:(g + 1) * blk]

    def total(slot, own=None):
        parts = [recv_v[slot, g].astype(jnp.float32) for g in range(ngroups) if own is None or g]
        if own is not None:
            parts = [own.astype(jnp.float32)] + parts
        full = (parts[0] + parts[1]) + (parts[2] + parts[3])
        return full * wet_v[...][None]

    def turn_tiles(k):
        def one(i, carry):
            s = k * per_chunk + i
            tiles_v[s] = tiles_v[s].T
            return carry

        lax.fori_loop(0, per_chunk, one, 0, unroll=8)

    @pl.when(month == last)
    def _():
        set_x(forcing_ref[...])
        for k in range(CHUNKS):
            tile_copy(k).wait()

            def run(i, carry):
                pair(k * (per_chunk // 2) + i, False)
                return carry

            lax.fori_loop(0, per_chunk // 2, run, 0, unroll=per_chunk // 2)
        gather_rows(0)
        meet()
        for g in range(ngroups):
            link(0, g, earlier).start()

        for k in range(CHUNKS):
            turn_tiles(k)

    @pl.when(month != last)
    def _():
        meet()
        for k in range(CHUNKS):
            tile_copy(k).wait()
            turn_tiles(k)

    def sweep_step(sweep, carry):
        @pl.when((month != last) | (sweep > 0))
        def _():
            for g in range(ngroups):
                arrival(sweep, g).wait_recv()
            state = total(sweep)
            set_x(state + forcing_ref[...])

            def run(i, carry):
                pair(i, True)
                return carry

            lax.fori_loop(0, slots // 2, run, 0, unroll=slots // 2)
            gather_rows(sweep)

            @pl.when((month == 0) & (sweep > 0))
            def _():
                for g in range(1, ngroups):
                    link(sweep, g, month).start()

            @pl.when((month != 0) | (sweep == 0))
            def _():
                for g in range(ngroups):
                    link(sweep, g, earlier).start()

            @pl.when((month != last) & (sweep > 0))
            def _():
                back_v[...] = state
                back(later).start()

        return carry

    lax.fori_loop(0, 2, sweep_step, 0)

    @pl.when(month == 0)
    def _():
        for g in range(1, ngroups):
            arrival(2, g).wait_recv()
        out_ref[...] = total(2, send_v[1, 0])
        for g in range(ngroups):
            link(0, g, earlier).wait_send()
        for g in range(1, ngroups):
            link(1, g, month).wait_send()

    @pl.when(month != 0)
    def _():
        for sweep in range(2):
            for g in range(ngroups):
                link(sweep, g, earlier).wait_send()
        back(later).wait_recv()

    @pl.when(month != last)
    def _():
        back(later).wait_send()


def on_device(forcing, tiles, tile_rows, tile_cols, tile_count, depth):
    months = lax.axis_size("month")
    ncols = lax.axis_size("cols")
    _, blk, tracers, block = forcing.shape
    slots = tiles.shape[1]
    pad = 8
    levels = block // depth.shape[1]
    dims = (months, ncols, blk, tracers, block, slots, levels)
    vmem = pl.BlockSpec(memory_space=pltpu.VMEM)
    smem = pl.BlockSpec(memory_space=pltpu.SMEM)
    result = pl.pallas_call(
        functools.partial(kernel, dims),
        out_shape=jax.ShapeDtypeStruct((tracers, blk, block), jnp.float32),
        in_specs=[smem, smem, vmem, vmem, vmem, pl.BlockSpec(memory_space=pltpu.HBM)],
        out_specs=vmem,
        scratch_shapes=[
            pltpu.VMEM((slots, block, block), jnp.bfloat16),
            pltpu.VMEM((blk, pad, block), jnp.float32),
            pltpu.VMEM((slots * pad, block), jnp.float32),
            pltpu.VMEM((4 * blk, slots), jnp.bfloat16),
            pltpu.VMEM((tracers, blk, block), jnp.float32),
            pltpu.VMEM((blk, block), jnp.float32),
            pltpu.VMEM((2, 4, tracers, blk, block), jnp.bfloat16),
            pltpu.VMEM((3, 4, tracers, blk, block), jnp.bfloat16),
            pltpu.SemaphoreType.DMA((CHUNKS,)),
            pltpu.SemaphoreType.DMA((2, 4)),
            pltpu.SemaphoreType.DMA((3, 4)),
            pltpu.SemaphoreType.DMA,
            pltpu.SemaphoreType.DMA,
        ],
        compiler_params=pltpu.CompilerParams(
            collective_id=0, has_side_effects=True, vmem_limit_bytes=56 << 20
        ),
        name="year_sweeps",
    )(tile_cols, tile_count, tile_rows, depth, jnp.swapaxes(forcing[0], 0, 1), tiles[0])
    return jnp.swapaxes(result, 0, 1)[None]


def solution(mesh):
    in_specs = (
        P("month", "cols", None, None),
        P("month", "cols", None, None),
        P("month", "cols"),
        P("month", "cols"),
        P("month", "cols"),
        P("cols", None),
    )
    out_specs = P("month", "cols", None, None)
    return jax.shard_map(
        on_device, mesh=mesh, in_specs=in_specs, out_specs=out_specs, check_vma=False
    )
```

```python
import functools

import jax
import jax.numpy as jnp
from jax import lax
from jax.experimental import pallas as pl
from jax.experimental.pallas import tpu as pltpu
from jax.sharding import PartitionSpec as P

MESH = pl.DeviceIdType.MESH
CHUNKS = 8
HALVES = 2


def kernel(
    dims,
    cols_ref,
    count_ref,
    rows_ref,
    depth_ref,
    forcing_ref,
    tiles_ref,
    out_ref,
    tiles_v,
    x_rows,
    terms,
    pick,
    back_v,
    wet_v,
    send_v,
    recv_v,
    tile_sem,
    send_sem,
    recv_sem,
    back_send,
    back_recv,
):
    months, ncols, blk, tracers, block, slots, levels = dims
    deltas = (0, ncols - 1, 1, ncols // 2)
    ngroups = len(deltas)
    pad = x_rows.shape[1]
    part = tracers // HALVES
    per_chunk = slots // CHUNKS
    month = lax.axis_index("month")
    here = lax.axis_index("cols")
    earlier = lax.rem(month + months - 1, months)
    later = lax.rem(month + 1, months)
    last = months - 1

    def tile_copy(k):
        part = pl.ds(k * per_chunk, per_chunk)
        return pltpu.make_async_copy(tiles_ref.at[part], tiles_v.at[part], tile_sem.at[k])

    for k in range(CHUNKS):
        tile_copy(k).start()

    barrier = pltpu.get_barrier_semaphore()

    def greet(other_month, delta):
        pl.semaphore_signal(
            barrier, inc=1,
            device_id={"month": other_month, "cols": lax.rem(here + delta, ncols)},
            device_id_type=MESH,
        )

    for delta in deltas:
        greet(later, delta)

    @pl.when(month == 0)
    def _():
        for delta in deltas[1:]:
            greet(month, delta)

    @pl.when(month != 0)
    def _():
        greet(earlier, 0)

    spread = (
        lax.broadcasted_iota(jnp.int32, (depth_ref.shape[1], block), 1) % depth_ref.shape[1]
        == lax.broadcasted_iota(jnp.int32, (depth_ref.shape[1], block), 0)
    ).astype(jnp.float32).astype(jnp.bfloat16)
    deep = jnp.dot(
        depth_ref[...].astype(jnp.float32).astype(jnp.bfloat16), spread,
        preferred_element_type=jnp.float32,
    )
    level = (lax.broadcasted_iota(jnp.int32, (blk, block), 1) // depth_ref.shape[1]).astype(jnp.float32)
    wet_v[...] = (level < deep).astype(jnp.float32)
    x_rows[...] = jnp.zeros_like(x_rows)
    live = lax.broadcasted_iota(jnp.int32, (blk, slots), 1) < count_ref[0, 0]
    inside = lax.broadcasted_iota(jnp.int32, (blk, slots), 0)
    for g, delta in enumerate(deltas):
        target = lax.rem(here + delta, ncols) * blk
        hit = ((inside + target) == rows_ref[...]) & live
        pick[g * blk:(g + 1) * blk, :] = hit.astype(jnp.float32).astype(jnp.bfloat16)

    def meet():
        @pl.when(month == 0)
        def _():
            pl.semaphore_wait(barrier, 2 * ngroups)

        @pl.when(month == last)
        def _():
            pl.semaphore_wait(barrier, ngroups)

        @pl.when((month != 0) & (month != last))
        def _():
            pl.semaphore_wait(barrier, ngroups + 1)

    def set_x(x):
        x = x.astype(jnp.bfloat16).astype(jnp.float32)
        for t in range(x.shape[0]):
            x_rows[:, t, :] = x[t]

    def pair(g, swapped):
        s = 2 * g
        zero = jnp.zeros((pad, block), jnp.float32)
        xa = x_rows[cols_ref[0, s] & (blk - 1)]
        xb = x_rows[cols_ref[0, s + 1] & (blk - 1)]
        lhs = jnp.concatenate(
            [
                jnp.concatenate([xa, zero], 0).astype(jnp.bfloat16),
                jnp.concatenate([zero, xb], 0).astype(jnp.bfloat16),
            ], 1,
        )
        two = tiles_v[pl.ds(s, 2)]
        if swapped:
            out = jnp.dot(lhs, two.reshape(2 * block, block), preferred_element_type=jnp.float32)
        else:
            out = lax.dot_general(
                lhs, jnp.concatenate([two[0], two[1]], 1), (((1,), (1,)), ((), ())),
                preferred_element_type=jnp.float32,
            )
        terms[pl.ds(s * pad, 2 * pad), :] = out

    def link(sweep, half, g, target_month):
        slot = sweep + (month == 0).astype(jnp.int32)
        return pltpu.make_async_remote_copy(
            src_ref=send_v.at[sweep, half, g],
            dst_ref=recv_v.at[slot, half, g],
            send_sem=send_sem.at[sweep, half, g],
            recv_sem=recv_sem.at[slot, half, g],
            device_id={"month": target_month, "cols": lax.rem(here + deltas[g], ncols)},
            device_id_type=MESH,
        )

    def arrival(slot, half, g):
        return pltpu.make_async_remote_copy(
            src_ref=send_v.at[0, half, g],
            dst_ref=recv_v.at[slot, half, g],
            send_sem=send_sem.at[0, half, g],
            recv_sem=recv_sem.at[slot, half, g],
            device_id={"month": earlier, "cols": here},
            device_id_type=MESH,
        )

    def send_all(sweep, half, target_month, groups):
        near_end = lax.rem(here, 4) == 3

        @pl.when(near_end)
        def _():
            for g in (2, 3, 1, 0):
                if g in groups:
                    link(sweep, half, g, target_month).start()

        @pl.when(jnp.logical_not(near_end))
        def _():
            for g in (1, 3, 2, 0):
                if g in groups:
                    link(sweep, half, g, target_month).start()

    def back(half):
        return pltpu.make_async_remote_copy(
            src_ref=back_v.at[half],
            dst_ref=out_ref.at[pl.ds(half * part, part)],
            send_sem=back_send.at[half],
            recv_sem=back_recv.at[half],
            device_id={"month": later, "cols": here},
            device_id_type=MESH,
        )

    def gather_rows(sweep, half, first):
        for t in range(part):
            terms_t = terms[pl.ds(first + t, slots, stride=pad), :].astype(jnp.bfloat16)
            rows_t = jnp.dot(pick[...], terms_t, preferred_element_type=jnp.float32)
            rows_t = rows_t.astype(jnp.bfloat16)
            for g in range(ngroups):
                send_v[sweep, half, g, t] = rows_t[g * blk:(g + 1) * blk]

    def total(slot, half, own=None):
        got = [recv_v[slot, half, g].astype(jnp.float32) for g in range(ngroups) if own is None or g]
        if own is not None:
            got = [own.astype(jnp.float32)] + got
        full = (got[0] + got[1]) + (got[2] + got[3])
        return full * wet_v[...][None]

    def turn_tiles(k):
        def one(i, carry):
            s = k * per_chunk + i
            tiles_v[s] = tiles_v[s].T
            return carry

        lax.fori_loop(0, per_chunk, one, 0, unroll=8)

    @pl.when(month == last)
    def _():
        set_x(forcing_ref[...])
        for k in range(CHUNKS):
            tile_copy(k).wait()

            def run(i, carry):
                pair(k * (per_chunk // 2) + i, False)
                return carry

            lax.fori_loop(0, per_chunk // 2, run, 0, unroll=per_chunk // 2)
        for half in range(HALVES):
            gather_rows(0, half, half * part)
            if half == 0:
                meet()
            send_all(0, half, earlier, range(ngroups))

        for k in range(CHUNKS):
            turn_tiles(k)

    @pl.when(month != last)
    def _():
        meet()
        for k in range(CHUNKS):
            tile_copy(k).wait()
            turn_tiles(k)

    def step(k, carry):
        sweep, half = k // HALVES, lax.rem(k, HALVES)

        @pl.when((month != last) | (sweep > 0))
        def _():
            for g in range(ngroups):
                arrival(sweep, half, g).wait_recv()
            state = total(sweep, half)
            set_x(state + forcing_ref[pl.ds(half * part, part)])

            def run(i, carry):
                pair(i, True)
                return carry

            lax.fori_loop(0, slots // 2, run, 0, unroll=slots // 2)
            gather_rows(sweep, half, 0)

            @pl.when((month == 0) & (sweep > 0))
            def _():
                send_all(sweep, half, month, range(1, ngroups))

            @pl.when((month != 0) | (sweep == 0))
            def _():
                send_all(sweep, half, earlier, range(ngroups))

            @pl.when((month != last) & (sweep > 0))
            def _():
                back_v[half] = total(sweep, half)
                back(half).start()

        return carry

    lax.fori_loop(0, 2 * HALVES, step, 0)

    @pl.when(month == 0)
    def _():
        for half in range(HALVES):
            for g in range(1, ngroups):
                arrival(2, half, g).wait_recv()
            out_ref[half * part:(half + 1) * part] = total(2, half, send_v[1, half, 0])
        for half in range(HALVES):
            for g in range(ngroups):
                link(0, half, g, earlier).wait_send()
            for g in range(1, ngroups):
                link(1, half, g, month).wait_send()

    @pl.when(month != 0)
    def _():
        for half in range(HALVES):
            for sweep in range(2):
                for g in range(ngroups):
                    link(sweep, half, g, earlier).wait_send()
            back(half).wait_recv()

    @pl.when(month != last)
    def _():
        for half in range(HALVES):
            back(half).wait_send()


def on_device(forcing, tiles, tile_rows, tile_cols, tile_count, depth):
    months = lax.axis_size("month")
    ncols = lax.axis_size("cols")
    _, blk, tracers, block = forcing.shape
    slots = tiles.shape[1]
    pad = 8
    part = tracers // HALVES
    levels = block // depth.shape[1]
    dims = (months, ncols, blk, tracers, block, slots, levels)
    vmem = pl.BlockSpec(memory_space=pltpu.VMEM)
    smem = pl.BlockSpec(memory_space=pltpu.SMEM)
    result = pl.pallas_call(
        functools.partial(kernel, dims),
        out_shape=jax.ShapeDtypeStruct((tracers, blk, block), jnp.float32),
        in_specs=[smem, smem, vmem, vmem, vmem, pl.BlockSpec(memory_space=pltpu.HBM)],
        out_specs=vmem,
        scratch_shapes=[
            pltpu.VMEM((slots, block, block), jnp.bfloat16),
            pltpu.VMEM((blk, pad, block), jnp.float32),
            pltpu.VMEM((slots * pad, block), jnp.float32),
            pltpu.VMEM((4 * blk, slots), jnp.bfloat16),
            pltpu.VMEM((HALVES, part, blk, block), jnp.float32),
            pltpu.VMEM((blk, block), jnp.float32),
            pltpu.VMEM((2, HALVES, 4, part, blk, block), jnp.bfloat16),
            pltpu.VMEM((3, HALVES, 4, part, blk, block), jnp.bfloat16),
            pltpu.SemaphoreType.DMA((CHUNKS,)),
            pltpu.SemaphoreType.DMA((2, HALVES, 4)),
            pltpu.SemaphoreType.DMA((3, HALVES, 4)),
            pltpu.SemaphoreType.DMA((HALVES,)),
            pltpu.SemaphoreType.DMA((HALVES,)),
        ],
        compiler_params=pltpu.CompilerParams(
            collective_id=0, has_side_effects=True, vmem_limit_bytes=56 << 20
        ),
        name="year_sweeps",
    )(tile_cols, tile_count, tile_rows, depth, jnp.swapaxes(forcing[0], 0, 1), tiles[0])
    return jnp.swapaxes(result, 0, 1)[None]


def solution(mesh):
    in_specs = (
        P("month", "cols", None, None),
        P("month", "cols", None, None),
        P("month", "cols"),
        P("month", "cols"),
        P("month", "cols"),
        P("cols", None),
    )
    out_specs = P("month", "cols", None, None)
    return jax.shard_map(
        on_device, mesh=mesh, in_specs=in_specs, out_specs=out_specs, check_vma=False
    )
```

```python
import functools

import jax
import jax.numpy as jnp
from jax import lax
from jax.experimental import pallas as pl
from jax.experimental.pallas import tpu as pltpu
from jax.sharding import PartitionSpec as P

MESH = pl.DeviceIdType.MESH
CHUNKS = 8
HALVES = 2


def kernel(
    dims,
    cols_ref,
    count_ref,
    rows_ref,
    depth_ref,
    forcing_ref,
    tiles_ref,
    out_ref,
    tiles_v,
    x_rows,
    terms,
    pick,
    force_v,
    wet_v,
    back_v,
    send_v,
    recv_v,
    cols_v,
    cols_w,
    tile_sem,
    send_sem,
    recv_sem,
    back_send,
    back_recv,
    hand_send,
    hand_recv,
    table_send,
    table_recv,
    cols_sem,
):
    months, ncols, blk, tracers, block, slots = dims
    deltas = (0, ncols - 1, 1, ncols // 2)
    ngroups = len(deltas)
    everyone = tuple(range(ngroups))
    pad = x_rows.shape[1]
    part = tracers // HALVES
    per_chunk = slots // CHUNKS
    month = lax.axis_index("month")
    here = lax.axis_index("cols")
    last = months - 1
    odd = lax.rem(month, 2) == 1
    even = jnp.logical_not(odd)

    def tile_copy(k):
        rows = pl.ds(k * per_chunk, per_chunk)
        return pltpu.make_async_copy(tiles_ref.at[rows], tiles_v.at[0, rows], tile_sem.at[k])

    for k in range(CHUNKS):
        tile_copy(k).start()
    own_cols = pltpu.make_async_copy(cols_ref, cols_v.at[0], cols_sem)
    own_cols.start()

    barrier = pltpu.get_barrier_semaphore()

    def greet(other_month, groups):
        for g in groups:
            pl.semaphore_signal(
                barrier, inc=1,
                device_id={"month": other_month, "cols": lax.rem(here + deltas[g], ncols)},
                device_id_type=MESH,
            )

    @pl.when(odd)
    def _():
        greet(lax.rem(month + 2, months), everyone)
        greet(month, everyone[1:])
        greet(month - 1, (0,))

    @pl.when(month == last - 2)
    def _():
        greet(last - 1, everyone)

    @pl.when(month == last - 1)
    def _():
        greet(last, everyone)

    @pl.when(month == 0)
    def _():
        greet(1, everyone)

    @pl.when(even & (month > 0))
    def _():
        greet(month - 1, (0,))

    def meet():
        cases = (
            (month == 1, 3 * ngroups),
            (odd & (month > 1) & (month < last), 2 * ngroups),
            (month == last, 3 * ngroups - 1),
            (month == last - 1, ngroups + 1),
            (even & (month < last - 1), 1),
        )
        for case, peers in cases:
            @pl.when(case)
            def _():
                pl.semaphore_wait(barrier, peers)

    spread = (
        lax.broadcasted_iota(jnp.int32, (depth_ref.shape[1], block), 1) % depth_ref.shape[1]
        == lax.broadcasted_iota(jnp.int32, (depth_ref.shape[1], block), 0)
    ).astype(jnp.float32).astype(jnp.bfloat16)
    deep = jnp.dot(
        depth_ref[...].astype(jnp.float32).astype(jnp.bfloat16), spread,
        preferred_element_type=jnp.float32,
    )
    level = (lax.broadcasted_iota(jnp.int32, (blk, block), 1) // depth_ref.shape[1]).astype(jnp.float32)
    wet_v[...] = (level < deep).astype(jnp.float32)
    force_v[0] = forcing_ref[...]
    x_rows[...] = jnp.zeros_like(x_rows)
    live = lax.broadcasted_iota(jnp.int32, (blk, slots), 1) < count_ref[0, 0]
    inside = lax.broadcasted_iota(jnp.int32, (blk, slots), 0)
    for g, delta in enumerate(deltas):
        target = lax.rem(here + delta, ncols) * blk
        hit = ((inside + target) == rows_ref[...]) & live
        pick[0, g * blk:(g + 1) * blk, :] = hit.astype(jnp.float32).astype(jnp.bfloat16)
    own_cols.wait()

    def set_x(x):
        x = x.astype(jnp.bfloat16).astype(jnp.float32)
        for t in range(x.shape[0]):
            x_rows[:, t, :] = x[t]

    def pair(g, held, swapped):
        s = 2 * g
        zero = jnp.zeros((pad, block), jnp.float32)
        xa = x_rows[cols_v[held, 0, s] & (blk - 1)]
        xb = x_rows[cols_v[held, 0, s + 1] & (blk - 1)]
        lhs = jnp.concatenate(
            [
                jnp.concatenate([xa, zero], 0).astype(jnp.bfloat16),
                jnp.concatenate([zero, xb], 0).astype(jnp.bfloat16),
            ], 1,
        )
        two = tiles_v[held, pl.ds(s, 2)]
        if swapped:
            out = jnp.dot(lhs, two.reshape(2 * block, block), preferred_element_type=jnp.float32)
        else:
            out = lax.dot_general(
                lhs, jnp.concatenate([two[0], two[1]], 1), (((1,), (1,)), ((), ())),
                preferred_element_type=jnp.float32,
            )
        terms[pl.ds(s * pad, 2 * pad), :] = out

    def link(turn, half, g, target_month, slot):
        return pltpu.make_async_remote_copy(
            src_ref=send_v.at[turn, half, g],
            dst_ref=recv_v.at[slot, half, g],
            send_sem=send_sem.at[turn, half, g],
            recv_sem=recv_sem.at[slot, half, g],
            device_id={"month": target_month, "cols": lax.rem(here + deltas[g], ncols)},
            device_id_type=MESH,
        )

    other = lax.rem(month + 2, months)

    def send_all(turn, half, target_month, slot, groups):
        near_end = lax.rem(here, 4) == 3

        @pl.when(near_end)
        def _():
            for g in (2, 3, 1, 0):
                if g in groups:
                    link(turn, half, g, target_month, slot).start()

        @pl.when(jnp.logical_not(near_end))
        def _():
            for g in (1, 3, 2, 0):
                if g in groups:
                    link(turn, half, g, target_month, slot).start()

    def back(half):
        return pltpu.make_async_remote_copy(
            src_ref=back_v.at[half],
            dst_ref=out_ref.at[pl.ds(half * part, part)],
            send_sem=back_send.at[half],
            recv_sem=back_recv.at[half],
            device_id={"month": lax.rem(month + 1, months), "cols": here},
            device_id_type=MESH,
        )

    def hand(source, dest, send, recv):
        return pltpu.make_async_remote_copy(
            src_ref=source, dst_ref=dest, send_sem=send, recv_sem=recv,
            device_id={"month": lax.rem(month + 1, months), "cols": here},
            device_id_type=MESH,
        )

    def hand_tiles(k):
        rows = pl.ds(k * per_chunk, per_chunk)
        return hand(tiles_v.at[0, rows], tiles_v.at[1, rows], hand_send.at[k], hand_recv.at[k])

    def hand_tables():
        return (
            hand(pick.at[0], pick.at[1], table_send.at[0], table_recv.at[0]),
            hand(force_v.at[0], force_v.at[1], table_send.at[1], table_recv.at[1]),
            hand(cols_ref, cols_w, table_send.at[2], table_recv.at[2]),
        )

    def gather_rows(held, turn, half, first):
        for t in range(part):
            terms_t = terms[pl.ds(first + t, slots, stride=pad), :].astype(jnp.bfloat16)
            rows_t = jnp.dot(pick[held], terms_t, preferred_element_type=jnp.float32)
            rows_t = rows_t.astype(jnp.bfloat16)
            for g in range(ngroups):
                send_v[turn, half, g, t] = rows_t[g * blk:(g + 1) * blk]

    def total(slot, half):
        got = [recv_v[slot, half, g].astype(jnp.float32) for g in range(ngroups)]
        full = (got[0] + got[1]) + (got[2] + got[3])
        return full * wet_v[...][None]

    def turn_tiles(k):
        def one(i, carry):
            s = k * per_chunk + i
            tiles_v[0, s] = tiles_v[0, s].T
            return carry

        lax.fori_loop(0, per_chunk, one, 0, unroll=8)

    @pl.when(month == last)
    def _():
        set_x(force_v[0])
        for k in range(CHUNKS):
            tile_copy(k).wait()

            def run(i, carry):
                pair(k * (per_chunk // 2) + i, 0, False)
                return carry

            lax.fori_loop(0, per_chunk // 2, run, 0, unroll=per_chunk // 2)
        for half in range(HALVES):
            gather_rows(0, 0, half, half * part)
            if half == 0:
                meet()
            send_all(0, half, last - 1, 0, everyone)

        for k in range(CHUNKS):
            turn_tiles(k)

    @pl.when(month == last - 1)
    def _():
        for k in range(CHUNKS):
            tile_copy(k).wait()
            turn_tiles(k)
        meet()
        for copy in hand_tables():
            copy.start()

    @pl.when(even & (month < last - 1))
    def _():
        for k in range(CHUNKS):
            tile_copy(k).wait()
            turn_tiles(k)
            if k == 0:
                meet()
                for copy in hand_tables():
                    copy.start()
            hand_tiles(k).start()

    @pl.when(odd & (month < last))
    def _():
        for k in range(CHUNKS):
            tile_copy(k).wait()
            turn_tiles(k)
        meet()

    def step(k, carry):
        sweep = k // (2 * HALVES)
        held = lax.rem(k // HALVES, 2)
        half = lax.rem(k, HALVES)
        turn = 2 * sweep + held
        opening = (month == last) & (sweep == 0)
        spare = (month == last - 1) & (turn == 0)
        took = jnp.where(month == last, 1, 0)

        @pl.when(odd & (held == 1) & (half == 0) & (sweep == took))
        def _():
            for copy in hand_tables():
                copy.wait_recv()
            pair_cols = pltpu.make_async_copy(cols_w, cols_v.at[1], cols_sem)
            pair_cols.start()
            for c in range(CHUNKS):
                hand_tiles(c).wait_recv()
            pair_cols.wait()

        @pl.when((odd & jnp.logical_not(opening)) | spare)
        def _():
            @pl.when(held == 0)
            def _():
                link(turn, half, 0, other, turn).wait_recv()

            @pl.when(held == 1)
            def _():
                recv_v[turn, half, 0] = send_v[turn - held, half, 0]

            for g in range(1, ngroups):
                link(turn, half, g, other, turn).wait_recv()
            state = total(turn, half)
            set_x(state + force_v[held, pl.ds(half * part, part)])

            def run(i, carry):
                pair(i, held, True)
                return carry

            lax.fori_loop(0, slots // 2, run, 0, unroll=slots // 2)
            gather_rows(held, turn, half, 0)

            @pl.when(spare)
            def _():
                send_all(turn, half, month - 1, 0, everyone)

            @pl.when(odd & (held == 0))
            def _():
                send_all(turn, half, month, turn + 1, everyone[1:])

            @pl.when(odd & (held == 1) & ((month > 1) | (sweep == 0)))
            def _():
                ahead = jnp.where(month == 1, 2, 0)
                send_all(turn, half, lax.rem(month + months - 2, months), 2 * sweep + ahead, everyone)

            @pl.when(odd & (held == 1) & (month == 1) & (sweep == 1))
            def _():
                send_all(turn, half, 0, 0, everyone)

            @pl.when((sweep == 1) & (held == 1))
            def _():
                out_ref[pl.ds(half * part, part)] = total(turn, half)

            @pl.when((sweep == 1) & (held == 0) & (month < last))
            def _():
                back_v[half] = total(turn, half)
                back(half).start()

        return carry

    lax.fori_loop(0, 4 * HALVES, step, 0)

    @pl.when(month == last - 1)
    def _():
        for k in range(CHUNKS):
            hand_tiles(k).start()

    @pl.when(month == 0)
    def _():
        for half in range(HALVES):
            for g in range(ngroups):
                link(0, half, g, other, 0).wait_recv()
            out_ref[half * part:(half + 1) * part] = total(0, half)

    @pl.when(even)
    def _():
        for copy in hand_tables():
            copy.wait_send()
        for k in range(CHUNKS):
            hand_tiles(k).wait_send()

    @pl.when(even & (month > 0))
    def _():
        for half in range(HALVES):
            back(half).wait_recv()

    @pl.when((month == last - 1) | (month == last))
    def _():
        for half in range(HALVES):
            for g in range(ngroups):
                link(0, half, g, other, 0).wait_send()

    @pl.when(odd & (month < last))
    def _():
        for half in range(HALVES):
            back(half).wait_send()
            for g in range(1, ngroups):
                link(0, half, g, other, 0).wait_send()
            for g in range(ngroups):
                link(1, half, g, other, 0).wait_send()

    @pl.when(odd)
    def _():
        for half in range(HALVES):
            for g in range(1, ngroups):
                link(2, half, g, other, 0).wait_send()
            for g in range(ngroups):
                link(3, half, g, other, 0).wait_send()


def on_device(forcing, tiles, tile_rows, tile_cols, tile_count, depth):
    months = lax.axis_size("month")
    ncols = lax.axis_size("cols")
    _, blk, tracers, block = forcing.shape
    slots = tiles.shape[1]
    pad = 8
    part = tracers // HALVES
    dims = (months, ncols, blk, tracers, block, slots)
    vmem = pl.BlockSpec(memory_space=pltpu.VMEM)
    smem = pl.BlockSpec(memory_space=pltpu.SMEM)
    result = pl.pallas_call(
        functools.partial(kernel, dims),
        out_shape=jax.ShapeDtypeStruct((tracers, blk, block), jnp.float32),
        in_specs=[vmem, smem, vmem, vmem, vmem, pl.BlockSpec(memory_space=pltpu.HBM)],
        out_specs=vmem,
        scratch_shapes=[
            pltpu.VMEM((2, slots, block, block), jnp.bfloat16),
            pltpu.VMEM((blk, pad, block), jnp.float32),
            pltpu.VMEM((slots * pad, block), jnp.float32),
            pltpu.VMEM((2, 4 * blk, slots), jnp.bfloat16),
            pltpu.VMEM((2, tracers, blk, block), jnp.float32),
            pltpu.VMEM((blk, block), jnp.float32),
            pltpu.VMEM((HALVES, part, blk, block), jnp.float32),
            pltpu.VMEM((4, HALVES, 4, part, blk, block), jnp.bfloat16),
            pltpu.VMEM((4, HALVES, 4, part, blk, block), jnp.bfloat16),
            pltpu.SMEM((2, 1, slots), jnp.int32),
            pltpu.VMEM((1, slots), jnp.int32),
            pltpu.SemaphoreType.DMA((CHUNKS,)),
            pltpu.SemaphoreType.DMA((4, HALVES, 4)),
            pltpu.SemaphoreType.DMA((4, HALVES, 4)),
            pltpu.SemaphoreType.DMA((HALVES,)),
            pltpu.SemaphoreType.DMA((HALVES,)),
            pltpu.SemaphoreType.DMA((CHUNKS,)),
            pltpu.SemaphoreType.DMA((CHUNKS,)),
            pltpu.SemaphoreType.DMA((3,)),
            pltpu.SemaphoreType.DMA((3,)),
            pltpu.SemaphoreType.DMA,
        ],
        compiler_params=pltpu.CompilerParams(
            collective_id=0, has_side_effects=True, vmem_limit_bytes=56 << 20
        ),
        name="year_sweeps",
    )(tile_cols, tile_count, tile_rows, depth, jnp.swapaxes(forcing[0], 0, 1), tiles[0])
    return jnp.swapaxes(result, 0, 1)[None]


def solution(mesh):
    in_specs = (
        P("month", "cols", None, None),
        P("month", "cols", None, None),
        P("month", "cols"),
        P("month", "cols"),
        P("month", "cols"),
        P("cols", None),
    )
    out_specs = P("month", "cols", None, None)
    return jax.shard_map(
        on_device, mesh=mesh, in_specs=in_specs, out_specs=out_specs, check_vma=False
    )
```

```python
import functools

import jax
import jax.numpy as jnp
from jax import lax
from jax.experimental import pallas as pl
from jax.experimental.pallas import tpu as pltpu
from jax.sharding import PartitionSpec as P

MESH = pl.DeviceIdType.MESH
CHUNKS = 8
HALVES = 2


def kernel(
    dims,
    cols_ref,
    count_ref,
    rows_ref,
    depth_ref,
    forcing_ref,
    tiles_ref,
    out_ref,
    tiles_v,
    x_rows,
    terms,
    pick,
    force_v,
    wet_v,
    back_v,
    send_v,
    recv_v,
    cols_v,
    cols_w,
    tile_sem,
    send_sem,
    recv_sem,
    back_send,
    back_recv,
    hand_send,
    hand_recv,
    table_send,
    table_recv,
    cols_sem,
):
    months, ncols, blk, tracers, block, slots = dims
    deltas = (0, ncols - 1, 1, ncols // 2)
    ngroups = len(deltas)
    everyone = tuple(range(ngroups))
    pad = x_rows.shape[1]
    part = tracers // HALVES
    per_chunk = slots // CHUNKS
    month = lax.axis_index("month")
    here = lax.axis_index("cols")
    last = months - 1
    odd = lax.rem(month, 2) == 1
    even = jnp.logical_not(odd)

    def tile_copy(k):
        rows = pl.ds(k * per_chunk, per_chunk)
        return pltpu.make_async_copy(tiles_ref.at[rows], tiles_v.at[0, rows], tile_sem.at[k])

    for k in range(CHUNKS):
        tile_copy(k).start()
    own_cols = pltpu.make_async_copy(cols_ref, cols_v.at[0], cols_sem)
    own_cols.start()

    barrier = pltpu.get_barrier_semaphore()

    def greet(other_month, groups):
        for g in groups:
            pl.semaphore_signal(
                barrier, inc=1,
                device_id={"month": other_month, "cols": lax.rem(here + deltas[g], ncols)},
                device_id_type=MESH,
            )

    @pl.when(odd)
    def _():
        greet(lax.rem(month + 2, months), everyone)
        greet(month, everyone[1:])
        greet(month - 1, (0,))

    @pl.when(month == last - 2)
    def _():
        greet(last - 1, everyone)

    @pl.when(month == last - 1)
    def _():
        greet(last, everyone)

    @pl.when(month == 0)
    def _():
        greet(1, everyone)

    @pl.when(even & (month > 0))
    def _():
        greet(month - 1, (0,))

    def meet():
        cases = (
            (month == 1, 3 * ngroups),
            (odd & (month > 1) & (month < last), 2 * ngroups),
            (month == last, 3 * ngroups - 1),
            (month == last - 1, ngroups + 1),
            (even & (month < last - 1), 1),
        )
        for case, peers in cases:
            @pl.when(case)
            def _():
                pl.semaphore_wait(barrier, peers)

    spread = (
        lax.broadcasted_iota(jnp.int32, (depth_ref.shape[1], block), 1) % depth_ref.shape[1]
        == lax.broadcasted_iota(jnp.int32, (depth_ref.shape[1], block), 0)
    ).astype(jnp.float32).astype(jnp.bfloat16)
    deep = jnp.dot(
        depth_ref[...].astype(jnp.float32).astype(jnp.bfloat16), spread,
        preferred_element_type=jnp.float32,
    )
    level = (lax.broadcasted_iota(jnp.int32, (blk, block), 1) // depth_ref.shape[1]).astype(jnp.float32)
    wet_v[...] = (level < deep).astype(jnp.float32)
    force_v[0] = forcing_ref[...]
    x_rows[...] = jnp.zeros_like(x_rows)
    live = lax.broadcasted_iota(jnp.int32, (blk, slots), 1) < count_ref[0, 0]
    inside = lax.broadcasted_iota(jnp.int32, (blk, slots), 0)
    for g, delta in enumerate(deltas):
        target = lax.rem(here + delta, ncols) * blk
        hit = ((inside + target) == rows_ref[...]) & live
        pick[0, g * blk:(g + 1) * blk, :] = hit.astype(jnp.float32).astype(jnp.bfloat16)
    own_cols.wait()

    def set_x(x):
        x = x.astype(jnp.bfloat16).astype(jnp.float32)
        for t in range(x.shape[0]):
            x_rows[:, t, :] = x[t]

    def pair(g, held, swapped):
        s = 2 * g
        zero = jnp.zeros((pad, block), jnp.float32)
        xa = x_rows[cols_v[held, 0, s] & (blk - 1)]
        xb = x_rows[cols_v[held, 0, s + 1] & (blk - 1)]
        lhs = jnp.concatenate(
            [
                jnp.concatenate([xa, zero], 0).astype(jnp.bfloat16),
                jnp.concatenate([zero, xb], 0).astype(jnp.bfloat16),
            ], 1,
        )
        two = tiles_v[held, pl.ds(s, 2)]
        if swapped:
            out = jnp.dot(lhs, two.reshape(2 * block, block), preferred_element_type=jnp.float32)
        else:
            out = lax.dot_general(
                lhs, jnp.concatenate([two[0], two[1]], 1), (((1,), (1,)), ((), ())),
                preferred_element_type=jnp.float32,
            )
        terms[pl.ds(s * pad, 2 * pad), :] = out

    def link(turn, half, g, target_month, slot):
        return pltpu.make_async_remote_copy(
            src_ref=send_v.at[turn, half, g],
            dst_ref=recv_v.at[slot, half, g],
            send_sem=send_sem.at[turn, half, g],
            recv_sem=recv_sem.at[slot, half, g],
            device_id={"month": target_month, "cols": lax.rem(here + deltas[g], ncols)},
            device_id_type=MESH,
        )

    other = lax.rem(month + 2, months)

    def send_all(turn, half, target_month, slot, groups):
        near_end = lax.rem(here, 4) == 3

        @pl.when(near_end)
        def _():
            for g in (2, 3, 1, 0):
                if g in groups:
                    link(turn, half, g, target_month, slot).start()

        @pl.when(jnp.logical_not(near_end))
        def _():
            for g in (1, 3, 2, 0):
                if g in groups:
                    link(turn, half, g, target_month, slot).start()

    def back(half):
        return pltpu.make_async_remote_copy(
            src_ref=back_v.at[half],
            dst_ref=out_ref.at[pl.ds(half * part, part)],
            send_sem=back_send.at[half],
            recv_sem=back_recv.at[half],
            device_id={"month": lax.rem(month + 1, months), "cols": here},
            device_id_type=MESH,
        )

    def hand(source, dest, send, recv):
        return pltpu.make_async_remote_copy(
            src_ref=source, dst_ref=dest, send_sem=send, recv_sem=recv,
            device_id={"month": lax.rem(month + 1, months), "cols": here},
            device_id_type=MESH,
        )

    def hand_tiles(k):
        rows = pl.ds(k * per_chunk, per_chunk)
        return hand(tiles_v.at[0, rows], tiles_v.at[1, rows], hand_send.at[k], hand_recv.at[k])

    def hand_tables():
        return (
            hand(pick.at[0], pick.at[1], table_send.at[0], table_recv.at[0]),
            hand(force_v.at[0], force_v.at[1], table_send.at[1], table_recv.at[1]),
            hand(cols_ref, cols_w, table_send.at[2], table_recv.at[2]),
        )

    def gather_rows(held, turn, half, first):
        columns = jnp.concatenate(
            [
                terms[pl.ds(first + t, slots, stride=pad), :].astype(jnp.bfloat16)
                for t in range(part)
            ], 1,
        )
        sums = jnp.dot(pick[held], columns, preferred_element_type=jnp.float32)
        sums = sums.astype(jnp.bfloat16)
        for t in range(part):
            for g in range(ngroups):
                send_v[turn, half, g, t] = sums[g * blk:(g + 1) * blk, t * block:(t + 1) * block]

    def total(slot, half):
        got = [recv_v[slot, half, g].astype(jnp.float32) for g in range(ngroups)]
        full = (got[0] + got[1]) + (got[2] + got[3])
        return full * wet_v[...][None]

    def turn_tiles(k):
        def one(i, carry):
            s = k * per_chunk + i
            tiles_v[0, s] = tiles_v[0, s].T
            return carry

        lax.fori_loop(0, per_chunk, one, 0, unroll=8)

    @pl.when(month == last)
    def _():
        set_x(force_v[0])
        for k in range(CHUNKS):
            tile_copy(k).wait()

            def run(i, carry):
                pair(k * (per_chunk // 2) + i, 0, False)
                return carry

            lax.fori_loop(0, per_chunk // 2, run, 0, unroll=per_chunk // 2)
        for half in range(HALVES):
            gather_rows(0, 0, half, half * part)
            if half == 0:
                meet()
            send_all(0, half, last - 1, 0, everyone)

        for k in range(CHUNKS):
            turn_tiles(k)

    @pl.when(month == last - 1)
    def _():
        for k in range(CHUNKS):
            tile_copy(k).wait()
            turn_tiles(k)
        meet()
        for copy in hand_tables():
            copy.start()

    @pl.when(even & (month < last - 1))
    def _():
        for k in range(CHUNKS):
            tile_copy(k).wait()
            turn_tiles(k)
            if k == 0:
                meet()
                for copy in hand_tables():
                    copy.start()
            hand_tiles(k).start()

    @pl.when(odd & (month < last))
    def _():
        for k in range(CHUNKS):
            tile_copy(k).wait()
            turn_tiles(k)
        meet()

    def step(k, carry):
        sweep = k // (2 * HALVES)
        held = lax.rem(k // HALVES, 2)
        half = lax.rem(k, HALVES)
        turn = 2 * sweep + held
        opening = (month == last) & (sweep == 0)
        spare = (month == last - 1) & (turn == 0)
        took = jnp.where(month == last, 1, 0)

        @pl.when(odd & (held == 1) & (half == 0) & (sweep == took))
        def _():
            for copy in hand_tables():
                copy.wait_recv()
            pair_cols = pltpu.make_async_copy(cols_w, cols_v.at[1], cols_sem)
            pair_cols.start()
            for c in range(CHUNKS):
                hand_tiles(c).wait_recv()
            pair_cols.wait()

        @pl.when((odd & jnp.logical_not(opening)) | spare)
        def _():
            @pl.when(held == 0)
            def _():
                link(turn, half, 0, other, turn).wait_recv()

            @pl.when(held == 1)
            def _():
                recv_v[turn, half, 0] = send_v[turn - held, half, 0]

            for g in range(1, ngroups):
                link(turn, half, g, other, turn).wait_recv()
            state = total(turn, half)
            set_x(state + force_v[held, pl.ds(half * part, part)])

            def run(i, carry):
                pair(i, held, True)
                return carry

            lax.fori_loop(0, slots // 2, run, 0, unroll=slots // 2)
            gather_rows(held, turn, half, 0)

            @pl.when(spare)
            def _():
                send_all(turn, half, month - 1, 0, everyone)

            @pl.when(odd & (held == 0))
            def _():
                send_all(turn, half, month, turn + 1, everyone[1:])

            @pl.when(odd & (held == 1) & ((month > 1) | (sweep == 0)))
            def _():
                ahead = jnp.where(month == 1, 2, 0)
                send_all(turn, half, lax.rem(month + months - 2, months), 2 * sweep + ahead, everyone)

            @pl.when(odd & (held == 1) & (month == 1) & (sweep == 1))
            def _():
                send_all(turn, half, 0, 0, everyone)

            @pl.when((sweep == 1) & (held == 1))
            def _():
                out_ref[pl.ds(half * part, part)] = total(turn, half)

            @pl.when((sweep == 1) & (held == 0) & (month < last))
            def _():
                back_v[half] = total(turn, half)
                back(half).start()

        return carry

    lax.fori_loop(0, 4 * HALVES, step, 0)

    @pl.when(month == last - 1)
    def _():
        for k in range(CHUNKS):
            hand_tiles(k).start()

    @pl.when(month == 0)
    def _():
        for half in range(HALVES):
            for g in range(ngroups):
                link(0, half, g, other, 0).wait_recv()
            out_ref[half * part:(half + 1) * part] = total(0, half)

    @pl.when(even)
    def _():
        for copy in hand_tables():
            copy.wait_send()
        for k in range(CHUNKS):
            hand_tiles(k).wait_send()

    @pl.when(even & (month > 0))
    def _():
        for half in range(HALVES):
            back(half).wait_recv()

    @pl.when((month == last - 1) | (month == last))
    def _():
        for half in range(HALVES):
            for g in range(ngroups):
                link(0, half, g, other, 0).wait_send()

    @pl.when(odd & (month < last))
    def _():
        for half in range(HALVES):
            back(half).wait_send()
            for g in range(1, ngroups):
                link(0, half, g, other, 0).wait_send()
            for g in range(ngroups):
                link(1, half, g, other, 0).wait_send()

    @pl.when(odd)
    def _():
        for half in range(HALVES):
            for g in range(1, ngroups):
                link(2, half, g, other, 0).wait_send()
            for g in range(ngroups):
                link(3, half, g, other, 0).wait_send()


def on_device(forcing, tiles, tile_rows, tile_cols, tile_count, depth):
    months = lax.axis_size("month")
    ncols = lax.axis_size("cols")
    _, blk, tracers, block = forcing.shape
    slots = tiles.shape[1]
    pad = 8
    part = tracers // HALVES
    dims = (months, ncols, blk, tracers, block, slots)
    vmem = pl.BlockSpec(memory_space=pltpu.VMEM)
    smem = pl.BlockSpec(memory_space=pltpu.SMEM)
    result = pl.pallas_call(
        functools.partial(kernel, dims),
        out_shape=pltpu.VMEM((tracers, blk, block), jnp.float32),
        in_specs=[vmem, smem, vmem, vmem, vmem, pl.BlockSpec(memory_space=pltpu.HBM)],
        out_specs=vmem,
        scratch_shapes=[
            pltpu.VMEM((2, slots, block, block), jnp.bfloat16),
            pltpu.VMEM((blk, pad, block), jnp.float32),
            pltpu.VMEM((slots * pad, block), jnp.float32),
            pltpu.VMEM((2, 4 * blk, slots), jnp.bfloat16),
            pltpu.VMEM((2, tracers, blk, block), jnp.float32),
            pltpu.VMEM((blk, block), jnp.float32),
            pltpu.VMEM((HALVES, part, blk, block), jnp.float32),
            pltpu.VMEM((4, HALVES, 4, part, blk, block), jnp.bfloat16),
            pltpu.VMEM((4, HALVES, 4, part, blk, block), jnp.bfloat16),
            pltpu.SMEM((2, 1, slots), jnp.int32),
            pltpu.VMEM((1, slots), jnp.int32),
            pltpu.SemaphoreType.DMA((CHUNKS,)),
            pltpu.SemaphoreType.DMA((4, HALVES, 4)),
            pltpu.SemaphoreType.DMA((4, HALVES, 4)),
            pltpu.SemaphoreType.DMA((HALVES,)),
            pltpu.SemaphoreType.DMA((HALVES,)),
            pltpu.SemaphoreType.DMA((CHUNKS,)),
            pltpu.SemaphoreType.DMA((CHUNKS,)),
            pltpu.SemaphoreType.DMA((3,)),
            pltpu.SemaphoreType.DMA((3,)),
            pltpu.SemaphoreType.DMA,
        ],
        compiler_params=pltpu.CompilerParams(
            collective_id=0, has_side_effects=True, vmem_limit_bytes=56 << 20
        ),
        name="year_sweeps",
    )(tile_cols, tile_count, tile_rows, depth, jnp.swapaxes(forcing[0], 0, 1), tiles[0])
    return jnp.swapaxes(result, 0, 1)[None]


def solution(mesh):
    in_specs = (
        P("month", "cols", None, None),
        P("month", "cols", None, None),
        P("month", "cols"),
        P("month", "cols"),
        P("month", "cols"),
        P("cols", None),
    )
    out_specs = P("month", "cols", None, None)
    return jax.shard_map(
        on_device, mesh=mesh, in_specs=in_specs, out_specs=out_specs, check_vma=False
    )
```

```python
import functools

import jax
import jax.numpy as jnp
from jax import lax
from jax.experimental import pallas as pl
from jax.experimental.pallas import tpu as pltpu
from jax.sharding import PartitionSpec as P

MESH = pl.DeviceIdType.MESH
CHUNKS = 4
HALVES = 2


def kernel(
    dims,
    cols_ref,
    count_ref,
    rows_ref,
    depth_ref,
    forcing_ref,
    tiles_ref,
    out_ref,
    tiles_v,
    x_rows,
    terms,
    pick,
    force_v,
    wet_v,
    back_v,
    send_v,
    recv_v,
    cols_v,
    cols_w,
    tile_sem,
    send_sem,
    recv_sem,
    back_send,
    back_recv,
    hand_send,
    hand_recv,
    table_send,
    table_recv,
    cols_sem,
):
    months, ncols, blk, tracers, block, slots = dims
    deltas = (0, ncols - 1, 1, ncols // 2)
    ngroups = len(deltas)
    everyone = tuple(range(ngroups))
    pad = x_rows.shape[1]
    part = tracers // HALVES
    per_chunk = slots // CHUNKS
    month = lax.axis_index("month")
    here = lax.axis_index("cols")
    last = months - 1
    odd = lax.rem(month, 2) == 1
    even = jnp.logical_not(odd)

    def tile_copy(k):
        rows = pl.ds(k * per_chunk, per_chunk)
        return pltpu.make_async_copy(tiles_ref.at[rows], tiles_v.at[0, rows], tile_sem.at[k])

    for k in range(CHUNKS):
        tile_copy(k).start()
    own_cols = pltpu.make_async_copy(cols_ref, cols_v.at[0], cols_sem)
    own_cols.start()

    barrier = pltpu.get_barrier_semaphore()

    def greet(other_month, groups):
        for g in groups:
            pl.semaphore_signal(
                barrier, inc=1,
                device_id={"month": other_month, "cols": lax.rem(here + deltas[g], ncols)},
                device_id_type=MESH,
            )

    @pl.when(odd)
    def _():
        greet(lax.rem(month + 2, months), everyone)
        greet(month, everyone[1:])
        greet(month - 1, (0,))

    @pl.when(month == last - 2)
    def _():
        greet(last - 1, everyone)

    @pl.when(month == last - 1)
    def _():
        greet(last, everyone)

    @pl.when(month == 0)
    def _():
        greet(1, everyone)

    @pl.when(even & (month > 0))
    def _():
        greet(month - 1, (0,))

    def meet():
        cases = (
            (month == 1, 3 * ngroups),
            (odd & (month > 1) & (month < last), 2 * ngroups),
            (month == last, 3 * ngroups - 1),
            (month == last - 1, ngroups + 1),
            (even & (month < last - 1), 1),
        )
        for case, peers in cases:
            @pl.when(case)
            def _():
                pl.semaphore_wait(barrier, peers)

    spread = (
        lax.broadcasted_iota(jnp.int32, (depth_ref.shape[1], block), 1) % depth_ref.shape[1]
        == lax.broadcasted_iota(jnp.int32, (depth_ref.shape[1], block), 0)
    ).astype(jnp.float32).astype(jnp.bfloat16)
    deep = jnp.dot(
        depth_ref[...].astype(jnp.float32).astype(jnp.bfloat16), spread,
        preferred_element_type=jnp.float32,
    )
    level = (lax.broadcasted_iota(jnp.int32, (blk, block), 1) // depth_ref.shape[1]).astype(jnp.float32)
    wet_v[...] = (level < deep).astype(jnp.float32)
    force_v[0] = forcing_ref[...]
    x_rows[...] = jnp.zeros_like(x_rows)
    live = lax.broadcasted_iota(jnp.int32, (blk, slots), 1) < count_ref[0, 0]
    inside = lax.broadcasted_iota(jnp.int32, (blk, slots), 0)
    for g, delta in enumerate(deltas):
        target = lax.rem(here + delta, ncols) * blk
        hit = ((inside + target) == rows_ref[...]) & live
        pick[0, g * blk:(g + 1) * blk, :] = hit.astype(jnp.float32).astype(jnp.bfloat16)
    own_cols.wait()

    def set_x(x):
        x = x.astype(jnp.bfloat16).astype(jnp.float32)
        for t in range(x.shape[0]):
            x_rows[:, t, :] = x[t]

    def pair(g, held, swapped):
        s = 2 * g
        zero = jnp.zeros((pad, block), jnp.float32)
        xa = x_rows[cols_v[held, 0, s] & (blk - 1)]
        xb = x_rows[cols_v[held, 0, s + 1] & (blk - 1)]
        lhs = jnp.concatenate(
            [
                jnp.concatenate([xa, zero], 0).astype(jnp.bfloat16),
                jnp.concatenate([zero, xb], 0).astype(jnp.bfloat16),
            ], 1,
        )
        two = tiles_v[held, pl.ds(s, 2)]
        if swapped:
            out = jnp.dot(lhs, two.reshape(2 * block, block), preferred_element_type=jnp.float32)
        else:
            out = lax.dot_general(
                lhs, jnp.concatenate([two[0], two[1]], 1), (((1,), (1,)), ((), ())),
                preferred_element_type=jnp.float32,
            )
        terms[pl.ds(s * pad, 2 * pad), :] = out

    def link(turn, half, g, target_month, slot):
        if isinstance(g, int):
            shift = deltas[g]
        else:
            shift = jnp.where(g == 1, ncols - 1, 1)
        return pltpu.make_async_remote_copy(
            src_ref=send_v.at[turn, half, g],
            dst_ref=recv_v.at[slot, half, g],
            send_sem=send_sem.at[turn, half, g],
            recv_sem=recv_sem.at[slot, half, g],
            device_id={"month": target_month, "cols": lax.rem(here + shift, ncols)},
            device_id_type=MESH,
        )

    other = lax.rem(month + 2, months)
    far = jnp.where(lax.rem(here, 4) == 3, 2, 1)

    def send_all(turn, half, target_month, slot, own):
        link(turn, half, far, target_month, slot).start()
        link(turn, half, 3, target_month, slot).start()
        link(turn, half, 3 - far, target_month, slot).start()
        if own is True:
            link(turn, half, 0, target_month, slot).start()
        else:
            @pl.when(own)
            def _():
                link(turn, half, 0, target_month, slot).start()

    def back(half):
        return pltpu.make_async_remote_copy(
            src_ref=back_v.at[half],
            dst_ref=out_ref.at[pl.ds(half * part, part)],
            send_sem=back_send.at[half],
            recv_sem=back_recv.at[half],
            device_id={"month": lax.rem(month + 1, months), "cols": here},
            device_id_type=MESH,
        )

    def hand(source, dest, send, recv):
        return pltpu.make_async_remote_copy(
            src_ref=source, dst_ref=dest, send_sem=send, recv_sem=recv,
            device_id={"month": lax.rem(month + 1, months), "cols": here},
            device_id_type=MESH,
        )

    def hand_tiles(k):
        rows = pl.ds(k * per_chunk, per_chunk)
        return hand(tiles_v.at[0, rows], tiles_v.at[1, rows], hand_send.at[k], hand_recv.at[k])

    def hand_tables():
        return (
            hand(pick.at[0], pick.at[1], table_send.at[0], table_recv.at[0]),
            hand(force_v.at[0], force_v.at[1], table_send.at[1], table_recv.at[1]),
            hand(cols_ref, cols_w, table_send.at[2], table_recv.at[2]),
        )

    def gather_rows(held, turn, half, first):
        columns = jnp.concatenate(
            [
                terms[pl.ds(first + t, slots, stride=pad), :].astype(jnp.bfloat16)
                for t in range(part)
            ], 1,
        )
        sums = jnp.dot(pick[held], columns, preferred_element_type=jnp.float32)
        sums = sums.astype(jnp.bfloat16)
        for t in range(part):
            for g in range(ngroups):
                send_v[turn, half, g, t] = sums[g * blk:(g + 1) * blk, t * block:(t + 1) * block]

    def total(slot, half):
        got = [recv_v[slot, half, g].astype(jnp.float32) for g in range(ngroups)]
        full = (got[0] + got[1]) + (got[2] + got[3])
        return full * wet_v[...][None]

    def turn_tiles(k):
        def one(i, carry):
            s = k * per_chunk + i
            tiles_v[0, s] = tiles_v[0, s].T
            return carry

        lax.fori_loop(0, per_chunk, one, 0, unroll=8)

    @pl.when(month == last)
    def _():
        set_x(force_v[0])
        for k in range(CHUNKS):
            tile_copy(k).wait()

            def run(i, carry):
                pair(k * (per_chunk // 2) + i, 0, False)
                return carry

            lax.fori_loop(0, per_chunk // 2, run, 0, unroll=per_chunk // 2)
        for half in range(HALVES):
            gather_rows(0, 0, half, half * part)
            if half == 0:
                meet()
            send_all(0, half, last - 1, 0, True)

        for k in range(CHUNKS):
            turn_tiles(k)

    @pl.when(month == last - 1)
    def _():
        for k in range(CHUNKS):
            tile_copy(k).wait()
            turn_tiles(k)
        meet()
        for copy in hand_tables():
            copy.start()

    @pl.when(even & (month < last - 1))
    def _():
        for k in range(CHUNKS):
            tile_copy(k).wait()
            turn_tiles(k)
            if k == 0:
                meet()
                for copy in hand_tables():
                    copy.start()
            hand_tiles(k).start()

    @pl.when(odd & (month < last))
    def _():
        for k in range(CHUNKS):
            tile_copy(k).wait()
            turn_tiles(k)
        meet()

    def step(k, carry):
        sweep = k // (2 * HALVES)
        held = lax.rem(k // HALVES, 2)
        half = lax.rem(k, HALVES)
        turn = 2 * sweep + held
        opening = (month == last) & (sweep == 0)
        spare = (month == last - 1) & (turn == 0)
        took = jnp.where(month == last, 1, 0)
        ending = (month == 1) & (turn == 3)
        onward = jnp.where(ending, 0, lax.rem(month + months - 2, months))
        goes_to = jnp.where(spare, month - 1, jnp.where(held == 0, month, onward))
        wraps = jnp.where((month == 1) & (turn == 1), 2, 0)
        lands = jnp.where(ending, 0, 2 * sweep + wraps)
        lands_in = jnp.where(spare, 0, jnp.where(held == 0, turn + 1, lands))

        @pl.when(odd & (held == 1) & (half == 0) & (sweep == took))
        def _():
            for copy in hand_tables():
                copy.wait_recv()
            pair_cols = pltpu.make_async_copy(cols_w, cols_v.at[1], cols_sem)
            pair_cols.start()
            for c in range(CHUNKS):
                hand_tiles(c).wait_recv()
            pair_cols.wait()

        @pl.when((odd & jnp.logical_not(opening)) | spare)
        def _():
            @pl.when(held == 0)
            def _():
                link(turn, half, 0, other, turn).wait_recv()

            @pl.when(held == 1)
            def _():
                recv_v[turn, half, 0] = send_v[turn - held, half, 0]

            for g in range(1, ngroups):
                link(turn, half, g, other, turn).wait_recv()
            state = total(turn, half)
            set_x(state + force_v[held, pl.ds(half * part, part)])

            def run(i, carry):
                pair(i, held, True)
                return carry

            lax.fori_loop(0, slots // 2, run, 0, unroll=slots // 2)
            gather_rows(held, turn, half, 0)

            send_all(turn, half, goes_to, lands_in, (held == 1) | spare)

            @pl.when((sweep == 1) & (held == 1))
            def _():
                out_ref[pl.ds(half * part, part)] = total(turn, half)

            @pl.when((sweep == 1) & (held == 0) & (month < last))
            def _():
                back_v[half] = total(turn, half)
                back(half).start()

        return carry

    lax.fori_loop(0, 4 * HALVES, step, 0)

    @pl.when(month == last - 1)
    def _():
        for k in range(CHUNKS):
            hand_tiles(k).start()

    @pl.when(month == 0)
    def _():
        for half in range(HALVES):
            for g in range(ngroups):
                link(0, half, g, other, 0).wait_recv()
            out_ref[half * part:(half + 1) * part] = total(0, half)

    @pl.when(even)
    def _():
        for copy in hand_tables():
            copy.wait_send()
        for k in range(CHUNKS):
            hand_tiles(k).wait_send()

    @pl.when(even & (month > 0))
    def _():
        for half in range(HALVES):
            back(half).wait_recv()

    @pl.when((month == last - 1) | (month == last))
    def _():
        for half in range(HALVES):
            for g in range(ngroups):
                link(0, half, g, other, 0).wait_send()

    @pl.when(odd & (month < last))
    def _():
        for half in range(HALVES):
            back(half).wait_send()
            for g in range(1, ngroups):
                link(0, half, g, other, 0).wait_send()
            for g in range(ngroups):
                link(1, half, g, other, 0).wait_send()

    @pl.when(odd)
    def _():
        for half in range(HALVES):
            for g in range(1, ngroups):
                link(2, half, g, other, 0).wait_send()
            for g in range(ngroups):
                link(3, half, g, other, 0).wait_send()


def on_device(forcing, tiles, tile_rows, tile_cols, tile_count, depth):
    months = lax.axis_size("month")
    ncols = lax.axis_size("cols")
    _, blk, tracers, block = forcing.shape
    slots = tiles.shape[1]
    pad = 8
    part = tracers // HALVES
    dims = (months, ncols, blk, tracers, block, slots)
    vmem = pl.BlockSpec(memory_space=pltpu.VMEM)
    smem = pl.BlockSpec(memory_space=pltpu.SMEM)
    result = pl.pallas_call(
        functools.partial(kernel, dims),
        out_shape=pltpu.VMEM((tracers, blk, block), jnp.float32),
        in_specs=[vmem, smem, vmem, vmem, vmem, pl.BlockSpec(memory_space=pltpu.HBM)],
        out_specs=vmem,
        scratch_shapes=[
            pltpu.VMEM((2, slots, block, block), jnp.bfloat16),
            pltpu.VMEM((blk, pad, block), jnp.float32),
            pltpu.VMEM((slots * pad, block), jnp.float32),
            pltpu.VMEM((2, 4 * blk, slots), jnp.bfloat16),
            pltpu.VMEM((2, tracers, blk, block), jnp.float32),
            pltpu.VMEM((blk, block), jnp.float32),
            pltpu.VMEM((HALVES, part, blk, block), jnp.float32),
            pltpu.VMEM((4, HALVES, 4, part, blk, block), jnp.bfloat16),
            pltpu.VMEM((4, HALVES, 4, part, blk, block), jnp.bfloat16),
            pltpu.SMEM((2, 1, slots), jnp.int32),
            pltpu.VMEM((1, slots), jnp.int32),
            pltpu.SemaphoreType.DMA((CHUNKS,)),
            pltpu.SemaphoreType.DMA((4, HALVES, 4)),
            pltpu.SemaphoreType.DMA((4, HALVES, 4)),
            pltpu.SemaphoreType.DMA((HALVES,)),
            pltpu.SemaphoreType.DMA((HALVES,)),
            pltpu.SemaphoreType.DMA((CHUNKS,)),
            pltpu.SemaphoreType.DMA((CHUNKS,)),
            pltpu.SemaphoreType.DMA((3,)),
            pltpu.SemaphoreType.DMA((3,)),
            pltpu.SemaphoreType.DMA,
        ],
        compiler_params=pltpu.CompilerParams(
            collective_id=0, has_side_effects=True, vmem_limit_bytes=56 << 20
        ),
        name="year_sweeps",
    )(tile_cols, tile_count, tile_rows, depth, jnp.swapaxes(forcing[0], 0, 1), tiles[0])
    return jnp.swapaxes(result, 0, 1)[None]


def solution(mesh):
    in_specs = (
        P("month", "cols", None, None),
        P("month", "cols", None, None),
        P("month", "cols"),
        P("month", "cols"),
        P("month", "cols"),
        P("cols", None),
    )
    out_specs = P("month", "cols", None, None)
    return jax.shard_map(
        on_device, mesh=mesh, in_specs=in_specs, out_specs=out_specs, check_vma=False
    )
```

```python
import functools

import jax
import jax.numpy as jnp
from jax import lax
from jax.experimental import pallas as pl
from jax.experimental.pallas import tpu as pltpu
from jax.sharding import PartitionSpec as P

MESH = pl.DeviceIdType.MESH
CHUNKS = 4
HALVES = 2


def kernel(
    dims,
    cols_ref,
    count_ref,
    rows_ref,
    depth_ref,
    forcing_ref,
    tiles_ref,
    out_ref,
    tiles_v,
    x_rows,
    terms,
    pick,
    force_v,
    wet_v,
    back_v,
    send_v,
    recv_v,
    cols_v,
    cols_w,
    tile_sem,
    send_sem,
    recv_sem,
    back_send,
    back_recv,
    hand_send,
    hand_recv,
    table_send,
    table_recv,
    cols_sem,
):
    months, ncols, blk, tracers, block, slots = dims
    deltas = (0, ncols - 1, 1, ncols // 2)
    ngroups = len(deltas)
    everyone = tuple(range(ngroups))
    pad = x_rows.shape[1]
    part = tracers // HALVES
    per_chunk = slots // CHUNKS
    month = lax.axis_index("month")
    here = lax.axis_index("cols")
    last = months - 1
    odd = lax.rem(month, 2) == 1
    even = jnp.logical_not(odd)

    def tile_copy(k):
        rows = pl.ds(k * per_chunk, per_chunk)
        return pltpu.make_async_copy(tiles_ref.at[rows], tiles_v.at[0, rows], tile_sem.at[k])

    for k in range(CHUNKS):
        tile_copy(k).start()
    own_cols = pltpu.make_async_copy(cols_ref, cols_v.at[0], cols_sem)
    own_cols.start()

    barrier = pltpu.get_barrier_semaphore()

    def greet(other_month, groups):
        for g in groups:
            pl.semaphore_signal(
                barrier, inc=1,
                device_id={"month": other_month, "cols": lax.rem(here + deltas[g], ncols)},
                device_id_type=MESH,
            )

    @pl.when(odd)
    def _():
        greet(lax.rem(month + 2, months), everyone)
        greet(month, everyone[1:])
        greet(month - 1, (0,))

    @pl.when(month == last - 2)
    def _():
        greet(last - 1, everyone)

    @pl.when(month == last - 1)
    def _():
        greet(last, everyone)

    @pl.when(month == 0)
    def _():
        greet(1, everyone)

    @pl.when(even & (month > 0))
    def _():
        greet(month - 1, (0,))

    def meet():
        cases = (
            (month == 1, 3 * ngroups),
            (odd & (month > 1) & (month < last), 2 * ngroups),
            (month == last, 3 * ngroups - 1),
            (month == last - 1, ngroups + 1),
            (even & (month < last - 1), 1),
        )
        for case, peers in cases:
            @pl.when(case)
            def _():
                pl.semaphore_wait(barrier, peers)

    spread = (
        lax.broadcasted_iota(jnp.int32, (depth_ref.shape[1], block), 1) % depth_ref.shape[1]
        == lax.broadcasted_iota(jnp.int32, (depth_ref.shape[1], block), 0)
    ).astype(jnp.float32).astype(jnp.bfloat16)
    deep = jnp.dot(
        depth_ref[...].astype(jnp.float32).astype(jnp.bfloat16), spread,
        preferred_element_type=jnp.float32,
    )
    level = (lax.broadcasted_iota(jnp.int32, (blk, block), 1) // depth_ref.shape[1]).astype(jnp.float32)
    wet_v[...] = (level < deep).astype(jnp.float32)
    force_v[0] = forcing_ref[...]
    x_rows[...] = jnp.zeros_like(x_rows)
    live = lax.broadcasted_iota(jnp.int32, (blk, slots), 1) < count_ref[0, 0]
    inside = lax.broadcasted_iota(jnp.int32, (blk, slots), 0)
    for g, delta in enumerate(deltas):
        target = lax.rem(here + delta, ncols) * blk
        hit = ((inside + target) == rows_ref[...]) & live
        pick[0, g * blk:(g + 1) * blk, :] = hit.astype(jnp.float32).astype(jnp.bfloat16)
    own_cols.wait()

    def set_x(x):
        x = x.astype(jnp.bfloat16).astype(jnp.float32)
        for t in range(x.shape[0]):
            x_rows[:, t, :] = x[t]

    def pair(g, held, swapped):
        s = 2 * g
        zero = jnp.zeros((pad, block), jnp.float32)
        xa = x_rows[cols_v[held, 0, s] & (blk - 1)]
        xb = x_rows[cols_v[held, 0, s + 1] & (blk - 1)]
        lhs = jnp.concatenate(
            [
                jnp.concatenate([xa, zero], 0).astype(jnp.bfloat16),
                jnp.concatenate([zero, xb], 0).astype(jnp.bfloat16),
            ], 1,
        )
        two = tiles_v[held, pl.ds(s, 2)]
        if swapped:
            out = jnp.dot(lhs, two.reshape(2 * block, block), preferred_element_type=jnp.float32)
        else:
            out = lax.dot_general(
                lhs, jnp.concatenate([two[0], two[1]], 1), (((1,), (1,)), ((), ())),
                preferred_element_type=jnp.float32,
            )
        terms[pl.ds(s * pad, 2 * pad), :] = out

    def link(turn, half, g, target_month, slot):
        if isinstance(g, int):
            shift = deltas[g]
        else:
            shift = jnp.where(g == 1, ncols - 1, 1)
        return pltpu.make_async_remote_copy(
            src_ref=send_v.at[turn, half, g],
            dst_ref=recv_v.at[slot, half, g],
            send_sem=send_sem.at[turn, half, g],
            recv_sem=recv_sem.at[slot, half, g],
            device_id={"month": target_month, "cols": lax.rem(here + shift, ncols)},
            device_id_type=MESH,
        )

    other = lax.rem(month + 2, months)
    far = jnp.where(lax.rem(here, 4) == 3, 2, 1)
    far_in = jnp.where(lax.rem(here, 4) == 0, 2, 1)

    def send_all(turn, half, target_month, slot, own):
        link(turn, half, far, target_month, slot).start()
        link(turn, half, 3, target_month, slot).start()
        link(turn, half, 3 - far, target_month, slot).start()
        if own is True:
            link(turn, half, 0, target_month, slot).start()
        else:
            @pl.when(own)
            def _():
                link(turn, half, 0, target_month, slot).start()

    def back(half):
        return pltpu.make_async_remote_copy(
            src_ref=back_v.at[half],
            dst_ref=out_ref.at[pl.ds(half * part, part)],
            send_sem=back_send.at[half],
            recv_sem=back_recv.at[half],
            device_id={"month": lax.rem(month + 1, months), "cols": here},
            device_id_type=MESH,
        )

    def hand(source, dest, send, recv):
        return pltpu.make_async_remote_copy(
            src_ref=source, dst_ref=dest, send_sem=send, recv_sem=recv,
            device_id={"month": lax.rem(month + 1, months), "cols": here},
            device_id_type=MESH,
        )

    def hand_tiles(k):
        rows = pl.ds(k * per_chunk, per_chunk)
        return hand(tiles_v.at[0, rows], tiles_v.at[1, rows], hand_send.at[k], hand_recv.at[k])

    def hand_tables():
        return (
            hand(pick.at[0], pick.at[1], table_send.at[0], table_recv.at[0]),
            hand(force_v.at[0], force_v.at[1], table_send.at[1], table_recv.at[1]),
            hand(cols_ref, cols_w, table_send.at[2], table_recv.at[2]),
        )

    def gather_rows(held, turn, half, first):
        columns = jnp.concatenate(
            [
                terms[pl.ds(first + t, slots, stride=pad), :].astype(jnp.bfloat16)
                for t in range(part)
            ], 1,
        )
        sums = jnp.dot(pick[held], columns, preferred_element_type=jnp.float32)
        sums = sums.astype(jnp.bfloat16)
        for t in range(part):
            for g in range(ngroups):
                send_v[turn, half, g, t] = sums[g * blk:(g + 1) * blk, t * block:(t + 1) * block]

    def total(slot, half):
        got = [recv_v[slot, half, g].astype(jnp.float32) for g in range(ngroups)]
        full = (got[0] + got[1]) + (got[2] + got[3])
        return full * wet_v[...][None]

    def turn_tiles(k):
        def one(i, carry):
            s = k * per_chunk + i
            tiles_v[0, s] = tiles_v[0, s].T
            return carry

        lax.fori_loop(0, per_chunk, one, 0, unroll=8)

    @pl.when(month == last)
    def _():
        set_x(force_v[0])
        for k in range(CHUNKS):
            tile_copy(k).wait()

            def run(i, carry):
                pair(k * (per_chunk // 2) + i, 0, False)
                return carry

            lax.fori_loop(0, per_chunk // 2, run, 0, unroll=per_chunk // 2)
        for half in range(HALVES):
            gather_rows(0, 0, half, half * part)
            if half == 0:
                meet()
            send_all(0, half, last - 1, 0, True)

        for k in range(CHUNKS):
            turn_tiles(k)

    @pl.when(month == last - 1)
    def _():
        for k in range(CHUNKS):
            tile_copy(k).wait()
            turn_tiles(k)
        meet()
        for copy in hand_tables():
            copy.start()

    @pl.when(even & (month < last - 1))
    def _():
        for k in range(CHUNKS):
            tile_copy(k).wait()
            turn_tiles(k)
            if k == 0:
                meet()
                for copy in hand_tables():
                    copy.start()
            hand_tiles(k).start()

    @pl.when(odd & (month < last))
    def _():
        for k in range(CHUNKS):
            tile_copy(k).wait()
            turn_tiles(k)
        meet()

    def step(k, carry):
        sweep = k // (2 * HALVES)
        held = lax.rem(k // HALVES, 2)
        half = lax.rem(k, HALVES)
        turn = 2 * sweep + held
        opening = (month == last) & (sweep == 0)
        spare = (month == last - 1) & (turn == 0)
        took = jnp.where(month == last, 1, 0)
        ending = (month == 1) & (turn == 3)
        onward = jnp.where(ending, 0, lax.rem(month + months - 2, months))
        goes_to = jnp.where(spare, month - 1, jnp.where(held == 0, month, onward))
        wraps = jnp.where((month == 1) & (turn == 1), 2, 0)
        lands = jnp.where(ending, 0, 2 * sweep + wraps)
        lands_in = jnp.where(spare, 0, jnp.where(held == 0, turn + 1, lands))

        @pl.when(odd & (held == 1) & (half == 0) & (sweep == took))
        def _():
            for copy in hand_tables():
                copy.wait_recv()
            pair_cols = pltpu.make_async_copy(cols_w, cols_v.at[1], cols_sem)
            pair_cols.start()
            for c in range(CHUNKS):
                hand_tiles(c).wait_recv()
            pair_cols.wait()

        @pl.when((odd & jnp.logical_not(opening)) | spare)
        def _():
            @pl.when(held == 0)
            def _():
                link(turn, half, 0, other, turn).wait_recv()

            @pl.when(held == 1)
            def _():
                recv_v[turn, half, 0] = send_v[turn - held, half, 0]

            for g in (3, 3 - far_in):
                link(turn, half, g, other, turn).wait_recv()
            near = (
                recv_v[turn, half, 0].astype(jnp.float32)
                + recv_v[turn, half, 3 - far_in].astype(jnp.float32)
            ) + recv_v[turn, half, 3].astype(jnp.float32)
            push = force_v[held, pl.ds(half * part, part)]
            link(turn, half, far_in, other, turn).wait_recv()
            state = (near + recv_v[turn, half, far_in].astype(jnp.float32)) * wet_v[...][None]
            set_x(state + push)

            def run(i, carry):
                pair(i, held, True)
                return carry

            lax.fori_loop(0, slots // 2, run, 0, unroll=slots // 2)
            gather_rows(held, turn, half, 0)

            send_all(turn, half, goes_to, lands_in, (held == 1) | spare)

            @pl.when((sweep == 1) & (held == 1))
            def _():
                out_ref[pl.ds(half * part, part)] = total(turn, half)

            @pl.when((sweep == 1) & (held == 0) & (month < last))
            def _():
                back_v[half] = total(turn, half)
                back(half).start()

        return carry

    lax.fori_loop(0, 4 * HALVES, step, 0)

    @pl.when(month == last - 1)
    def _():
        for k in range(CHUNKS):
            hand_tiles(k).start()

    @pl.when(month == 0)
    def _():
        for half in range(HALVES):
            for g in range(ngroups):
                link(0, half, g, other, 0).wait_recv()
            out_ref[half * part:(half + 1) * part] = total(0, half)

    @pl.when(even)
    def _():
        for copy in hand_tables():
            copy.wait_send()
        for k in range(CHUNKS):
            hand_tiles(k).wait_send()

    @pl.when(even & (month > 0))
    def _():
        for half in range(HALVES):
            back(half).wait_recv()

    @pl.when((month == last - 1) | (month == last))
    def _():
        for half in range(HALVES):
            for g in range(ngroups):
                link(0, half, g, other, 0).wait_send()

    @pl.when(odd & (month < last))
    def _():
        for half in range(HALVES):
            back(half).wait_send()
            for g in range(1, ngroups):
                link(0, half, g, other, 0).wait_send()
            for g in range(ngroups):
                link(1, half, g, other, 0).wait_send()

    @pl.when(odd)
    def _():
        for half in range(HALVES):
            for g in range(1, ngroups):
                link(2, half, g, other, 0).wait_send()
            for g in range(ngroups):
                link(3, half, g, other, 0).wait_send()


def on_device(forcing, tiles, tile_rows, tile_cols, tile_count, depth):
    months = lax.axis_size("month")
    ncols = lax.axis_size("cols")
    _, blk, tracers, block = forcing.shape
    slots = tiles.shape[1]
    pad = 8
    part = tracers // HALVES
    dims = (months, ncols, blk, tracers, block, slots)
    vmem = pl.BlockSpec(memory_space=pltpu.VMEM)
    smem = pl.BlockSpec(memory_space=pltpu.SMEM)
    result = pl.pallas_call(
        functools.partial(kernel, dims),
        out_shape=pltpu.VMEM((tracers, blk, block), jnp.float32),
        in_specs=[vmem, smem, vmem, vmem, vmem, pl.BlockSpec(memory_space=pltpu.HBM)],
        out_specs=vmem,
        scratch_shapes=[
            pltpu.VMEM((2, slots, block, block), jnp.bfloat16),
            pltpu.VMEM((blk, pad, block), jnp.float32),
            pltpu.VMEM((slots * pad, block), jnp.float32),
            pltpu.VMEM((2, 4 * blk, slots), jnp.bfloat16),
            pltpu.VMEM((2, tracers, blk, block), jnp.float32),
            pltpu.VMEM((blk, block), jnp.float32),
            pltpu.VMEM((HALVES, part, blk, block), jnp.float32),
            pltpu.VMEM((4, HALVES, 4, part, blk, block), jnp.bfloat16),
            pltpu.VMEM((4, HALVES, 4, part, blk, block), jnp.bfloat16),
            pltpu.SMEM((2, 1, slots), jnp.int32),
            pltpu.VMEM((1, slots), jnp.int32),
            pltpu.SemaphoreType.DMA((CHUNKS,)),
            pltpu.SemaphoreType.DMA((4, HALVES, 4)),
            pltpu.SemaphoreType.DMA((4, HALVES, 4)),
            pltpu.SemaphoreType.DMA((HALVES,)),
            pltpu.SemaphoreType.DMA((HALVES,)),
            pltpu.SemaphoreType.DMA((CHUNKS,)),
            pltpu.SemaphoreType.DMA((CHUNKS,)),
            pltpu.SemaphoreType.DMA((3,)),
            pltpu.SemaphoreType.DMA((3,)),
            pltpu.SemaphoreType.DMA,
        ],
        compiler_params=pltpu.CompilerParams(
            collective_id=0, has_side_effects=True, vmem_limit_bytes=56 << 20
        ),
        name="year_sweeps",
    )(tile_cols, tile_count, tile_rows, depth, jnp.swapaxes(forcing[0], 0, 1), tiles[0])
    return jnp.swapaxes(result, 0, 1)[None]


def solution(mesh):
    in_specs = (
        P("month", "cols", None, None),
        P("month", "cols", None, None),
        P("month", "cols"),
        P("month", "cols"),
        P("month", "cols"),
        P("cols", None),
    )
    out_specs = P("month", "cols", None, None)
    return jax.shard_map(
        on_device, mesh=mesh, in_specs=in_specs, out_specs=out_specs, check_vma=False
    )
```

```python
import functools

import jax
import jax.numpy as jnp
from jax import lax
from jax.experimental import pallas as pl
from jax.experimental.pallas import tpu as pltpu
from jax.sharding import PartitionSpec as P

MESH = pl.DeviceIdType.MESH
CHUNKS = 4
HALVES = 2


def kernel(
    dims,
    cols_ref,
    count_ref,
    rows_ref,
    depth_ref,
    forcing_ref,
    tiles_ref,
    out_ref,
    tiles_v,
    x_rows,
    terms,
    pick,
    force_v,
    wet_v,
    back_v,
    send_v,
    recv_v,
    cols_v,
    cols_w,
    tile_sem,
    send_sem,
    recv_sem,
    back_send,
    back_recv,
    hand_send,
    hand_recv,
    table_send,
    table_recv,
    cols_sem,
):
    months, ncols, blk, tracers, block, slots = dims
    deltas = (0, ncols - 1, 1, ncols // 2)
    ngroups = len(deltas)
    everyone = tuple(range(ngroups))
    pad = x_rows.shape[1]
    part = tracers // HALVES
    per_chunk = slots // CHUNKS
    month = lax.axis_index("month")
    here = lax.axis_index("cols")
    last = months - 1
    odd = lax.rem(month, 2) == 1
    even = jnp.logical_not(odd)

    def tile_copy(k):
        rows = pl.ds(k * per_chunk, per_chunk)
        return pltpu.make_async_copy(tiles_ref.at[rows], tiles_v.at[0, rows], tile_sem.at[k])

    for k in range(CHUNKS):
        tile_copy(k).start()
    own_cols = pltpu.make_async_copy(cols_ref, cols_v.at[0], cols_sem)
    own_cols.start()

    barrier = pltpu.get_barrier_semaphore()

    def greet(other_month, groups):
        for g in groups:
            pl.semaphore_signal(
                barrier, inc=1,
                device_id={"month": other_month, "cols": lax.rem(here + deltas[g], ncols)},
                device_id_type=MESH,
            )

    @pl.when(odd)
    def _():
        greet(lax.rem(month + 2, months), everyone)
        greet(month, everyone[1:])
        greet(month - 1, (0,))

    @pl.when(month == last - 2)
    def _():
        greet(last - 1, everyone)

    @pl.when(month == last - 1)
    def _():
        greet(last, everyone)

    @pl.when(month == 0)
    def _():
        greet(1, everyone)

    @pl.when(even & (month > 0))
    def _():
        greet(month - 1, (0,))

    def meet():
        cases = (
            (month == 1, 3 * ngroups),
            (odd & (month > 1) & (month < last), 2 * ngroups),
            (month == last, 3 * ngroups - 1),
            (month == last - 1, ngroups + 1),
            (even & (month < last - 1), 1),
        )
        for case, peers in cases:
            @pl.when(case)
            def _():
                pl.semaphore_wait(barrier, peers)

    spread = (
        lax.broadcasted_iota(jnp.int32, (depth_ref.shape[1], block), 1) % depth_ref.shape[1]
        == lax.broadcasted_iota(jnp.int32, (depth_ref.shape[1], block), 0)
    ).astype(jnp.float32).astype(jnp.bfloat16)
    deep = jnp.dot(
        depth_ref[...].astype(jnp.float32).astype(jnp.bfloat16), spread,
        preferred_element_type=jnp.float32,
    )
    level = (lax.broadcasted_iota(jnp.int32, (blk, block), 1) // depth_ref.shape[1]).astype(jnp.float32)
    wet_v[...] = (level < deep).astype(jnp.float32)
    force_v[0] = forcing_ref[...]
    x_rows[...] = jnp.zeros_like(x_rows)
    live = lax.broadcasted_iota(jnp.int32, (blk, slots), 1) < count_ref[0, 0]
    inside = lax.broadcasted_iota(jnp.int32, (blk, slots), 0)
    for g, delta in enumerate(deltas):
        target = lax.rem(here + delta, ncols) * blk
        hit = ((inside + target) == rows_ref[...]) & live
        pick[0, g * blk:(g + 1) * blk, :] = hit.astype(jnp.float32).astype(jnp.bfloat16)
    own_cols.wait()

    def set_x(x):
        x = x.astype(jnp.bfloat16).astype(jnp.float32)
        for t in range(x.shape[0]):
            x_rows[0:blk, t, :] = x[t]

    def pair(g, held, swapped):
        s = 2 * g
        zero = jnp.zeros((pad, block), jnp.float32)
        xa = x_rows[cols_v[held, 0, s] & (blk - 1)]
        xb = x_rows[cols_v[held, 0, s + 1] & (blk - 1)]
        lhs = jnp.concatenate(
            [
                jnp.concatenate([xa, zero], 0).astype(jnp.bfloat16),
                jnp.concatenate([zero, xb], 0).astype(jnp.bfloat16),
            ], 1,
        )
        two = tiles_v[held, pl.ds(s, 2)]
        if swapped:
            out = jnp.dot(lhs, two.reshape(2 * block, block), preferred_element_type=jnp.float32)
        else:
            out = lax.dot_general(
                lhs, jnp.concatenate([two[0], two[1]], 1), (((1,), (1,)), ((), ())),
                preferred_element_type=jnp.float32,
            )
        terms[pl.ds(s * pad, 2 * pad), :] = out

    def link(turn, half, g, target_month, slot):
        if isinstance(g, int):
            shift = deltas[g]
        else:
            shift = jnp.where(g == 1, ncols - 1, 1)
        return pltpu.make_async_remote_copy(
            src_ref=send_v.at[turn, half, g],
            dst_ref=recv_v.at[slot, half, g],
            send_sem=send_sem.at[turn, half, g],
            recv_sem=recv_sem.at[slot, half, g],
            device_id={"month": target_month, "cols": lax.rem(here + shift, ncols)},
            device_id_type=MESH,
        )

    other = lax.rem(month + 2, months)
    far = jnp.where(lax.rem(here, 4) == 3, 2, 1)
    far_in = jnp.where(lax.rem(here, 4) == 0, 2, 1)

    def send_all(turn, half, target_month, slot, own):
        link(turn, half, far, target_month, slot).start()
        link(turn, half, 3, target_month, slot).start()
        link(turn, half, 3 - far, target_month, slot).start()
        if own is True:
            link(turn, half, 0, target_month, slot).start()
        else:
            @pl.when(own)
            def _():
                link(turn, half, 0, target_month, slot).start()

    def back(half):
        return pltpu.make_async_remote_copy(
            src_ref=back_v.at[half],
            dst_ref=out_ref.at[pl.ds(half * part, part)],
            send_sem=back_send.at[half],
            recv_sem=back_recv.at[half],
            device_id={"month": lax.rem(month + 1, months), "cols": here},
            device_id_type=MESH,
        )

    def hand(source, dest, send, recv):
        return pltpu.make_async_remote_copy(
            src_ref=source, dst_ref=dest, send_sem=send, recv_sem=recv,
            device_id={"month": lax.rem(month + 1, months), "cols": here},
            device_id_type=MESH,
        )

    def hand_tiles(k):
        rows = pl.ds(k * per_chunk, per_chunk)
        return hand(tiles_v.at[0, rows], tiles_v.at[1, rows], hand_send.at[k], hand_recv.at[k])

    def hand_tables():
        return (
            hand(pick.at[0], pick.at[1], table_send.at[0], table_recv.at[0]),
            hand(force_v.at[0], force_v.at[1], table_send.at[1], table_recv.at[1]),
            hand(cols_ref, cols_w, table_send.at[2], table_recv.at[2]),
        )

    def gather_rows(held, turn, half, first):
        columns = jnp.concatenate(
            [
                terms[pl.ds(first + t, slots, stride=pad), :].astype(jnp.bfloat16)
                for t in range(part)
            ], 1,
        )
        sums = jnp.dot(pick[held], columns, preferred_element_type=jnp.float32)
        sums = sums.astype(jnp.bfloat16)
        for t in range(part):
            for g in range(ngroups):
                send_v[turn, half, g, t] = sums[g * blk:(g + 1) * blk, t * block:(t + 1) * block]

    def total(slot, half):
        got = [recv_v[slot, half, g].astype(jnp.float32) for g in range(ngroups)]
        full = (got[0] + got[1]) + (got[2] + got[3])
        return full * wet_v[...][None]

    def turn_tiles(k):
        def one(i, carry):
            s = k * per_chunk + i
            tiles_v[0, s] = tiles_v[0, s].T
            return carry

        lax.fori_loop(0, per_chunk, one, 0, unroll=8)

    @pl.when(month == last)
    def _():
        set_x(force_v[0])
        for k in range(CHUNKS):
            tile_copy(k).wait()

            def run(i, carry):
                pair(k * (per_chunk // 2) + i, 0, False)
                return carry

            lax.fori_loop(0, per_chunk // 2, run, 0, unroll=per_chunk // 2)
        for half in range(HALVES):
            gather_rows(0, 0, half, half * part)
            if half == 0:
                meet()
            send_all(0, half, last - 1, 0, True)

        for k in range(CHUNKS):
            turn_tiles(k)

    @pl.when(month == last - 1)
    def _():
        for k in range(CHUNKS):
            tile_copy(k).wait()
            turn_tiles(k)
        meet()
        for copy in hand_tables():
            copy.start()

    @pl.when(even & (month < last - 1))
    def _():
        for k in range(CHUNKS):
            tile_copy(k).wait()
            turn_tiles(k)
            if k == 0:
                meet()
                for copy in hand_tables():
                    copy.start()
            hand_tiles(k).start()

    @pl.when(odd & (month < last))
    def _():
        for k in range(CHUNKS):
            tile_copy(k).wait()
            turn_tiles(k)
        meet()

    def step(k, carry):
        sweep = k // (2 * HALVES)
        held = lax.rem(k // HALVES, 2)
        half = lax.rem(k, HALVES)
        turn = 2 * sweep + held
        opening = (month == last) & (sweep == 0)
        spare = (month == last - 1) & (turn == 0)
        took = jnp.where(month == last, 1, 0)
        ending = (month == 1) & (turn == 3)
        onward = jnp.where(ending, 0, lax.rem(month + months - 2, months))
        goes_to = jnp.where(spare, month - 1, jnp.where(held == 0, month, onward))
        wraps = jnp.where((month == 1) & (turn == 1), 2, 0)
        lands = jnp.where(ending, 0, 2 * sweep + wraps)
        lands_in = jnp.where(spare, 0, jnp.where(held == 0, turn + 1, lands))

        @pl.when(odd & (held == 1) & (half == 0) & (sweep == took))
        def _():
            for copy in hand_tables():
                copy.wait_recv()
            pair_cols = pltpu.make_async_copy(cols_w, cols_v.at[1], cols_sem)
            pair_cols.start()
            for c in range(CHUNKS):
                hand_tiles(c).wait_recv()
            pair_cols.wait()

        @pl.when((odd & jnp.logical_not(opening)) | spare)
        def _():
            @pl.when(held == 0)
            def _():
                link(turn, half, 0, other, turn).wait_recv()

            @pl.when(held == 1)
            def _():
                recv_v[turn, half, 0] = send_v[turn - held, half, 0]

            for g in (3, 3 - far_in):
                link(turn, half, g, other, turn).wait_recv()
            near = (
                recv_v[turn, half, 0].astype(jnp.float32)
                + recv_v[turn, half, 3 - far_in].astype(jnp.float32)
            ) + recv_v[turn, half, 3].astype(jnp.float32)
            push = force_v[held, pl.ds(half * part, part)]
            link(turn, half, far_in, other, turn).wait_recv()
            state = (near + recv_v[turn, half, far_in].astype(jnp.float32)) * wet_v[...][None]
            set_x(state + push)

            def run(i, carry):
                pair(i, held, True)
                return carry

            lax.fori_loop(0, slots // 2, run, 0, unroll=slots // 2)
            gather_rows(held, turn, half, 0)

            send_all(turn, half, goes_to, lands_in, (held == 1) | spare)

            @pl.when((sweep == 1) & (held == 1))
            def _():
                out_ref[pl.ds(half * part, part)] = total(turn, half)

            @pl.when((sweep == 1) & (held == 0) & (month < last))
            def _():
                back_v[half] = total(turn, half)
                back(half).start()

        return carry

    lax.fori_loop(0, 4 * HALVES, step, 0)

    @pl.when(month == last - 1)
    def _():
        for k in range(CHUNKS):
            hand_tiles(k).start()

    @pl.when(month == 0)
    def _():
        for half in range(HALVES):
            for g in range(ngroups):
                link(0, half, g, other, 0).wait_recv()
            out_ref[half * part:(half + 1) * part] = total(0, half)

    @pl.when(even)
    def _():
        for copy in hand_tables():
            copy.wait_send()
        for k in range(CHUNKS):
            hand_tiles(k).wait_send()

    @pl.when(even & (month > 0))
    def _():
        for half in range(HALVES):
            back(half).wait_recv()

    @pl.when((month == last - 1) | (month == last))
    def _():
        for half in range(HALVES):
            for g in range(ngroups):
                link(0, half, g, other, 0).wait_send()

    @pl.when(odd & (month < last))
    def _():
        for half in range(HALVES):
            back(half).wait_send()
            for g in range(1, ngroups):
                link(0, half, g, other, 0).wait_send()
            for g in range(ngroups):
                link(1, half, g, other, 0).wait_send()

    @pl.when(odd)
    def _():
        for half in range(HALVES):
            for g in range(1, ngroups):
                link(2, half, g, other, 0).wait_send()
            for g in range(ngroups):
                link(3, half, g, other, 0).wait_send()


def on_device(forcing, tiles, tile_rows, tile_cols, tile_count, depth):
    months = lax.axis_size("month")
    ncols = lax.axis_size("cols")
    _, blk, tracers, block = forcing.shape
    slots = tiles.shape[1]
    pad = 8
    part = tracers // HALVES
    dims = (months, ncols, blk, tracers, block, slots)
    vmem = pl.BlockSpec(memory_space=pltpu.VMEM)
    smem = pl.BlockSpec(memory_space=pltpu.SMEM)
    result = pl.pallas_call(
        functools.partial(kernel, dims),
        out_shape=pltpu.VMEM((tracers, blk, block), jnp.float32),
        in_specs=[vmem, smem, vmem, vmem, vmem, pl.BlockSpec(memory_space=pltpu.HBM)],
        out_specs=vmem,
        scratch_shapes=[
            pltpu.VMEM((2, slots, block, block), jnp.bfloat16),
            pltpu.VMEM((blk + 1, pad, block), jnp.float32),
            pltpu.VMEM((slots * pad + pad, block), jnp.float32),
            pltpu.VMEM((2, 4 * blk, slots), jnp.bfloat16),
            pltpu.VMEM((2, tracers, blk, block), jnp.float32),
            pltpu.VMEM((blk, block), jnp.float32),
            pltpu.VMEM((HALVES, part, blk, block), jnp.float32),
            pltpu.VMEM((4, HALVES, 4, part, blk, block), jnp.bfloat16),
            pltpu.VMEM((4, HALVES, 4, part, blk, block), jnp.bfloat16),
            pltpu.SMEM((2, 1, slots), jnp.int32),
            pltpu.VMEM((1, slots), jnp.int32),
            pltpu.SemaphoreType.DMA((CHUNKS,)),
            pltpu.SemaphoreType.DMA((4, HALVES, 4)),
            pltpu.SemaphoreType.DMA((4, HALVES, 4)),
            pltpu.SemaphoreType.DMA((HALVES,)),
            pltpu.SemaphoreType.DMA((HALVES,)),
            pltpu.SemaphoreType.DMA((CHUNKS,)),
            pltpu.SemaphoreType.DMA((CHUNKS,)),
            pltpu.SemaphoreType.DMA((3,)),
            pltpu.SemaphoreType.DMA((3,)),
            pltpu.SemaphoreType.DMA,
        ],
        compiler_params=pltpu.CompilerParams(
            collective_id=0, has_side_effects=True, vmem_limit_bytes=56 << 20
        ),
        name="year_sweeps",
    )(tile_cols, tile_count, tile_rows, depth, jnp.swapaxes(forcing[0], 0, 1), tiles[0])
    return jnp.swapaxes(result, 0, 1)[None]


def solution(mesh):
    in_specs = (
        P("month", "cols", None, None),
        P("month", "cols", None, None),
        P("month", "cols"),
        P("month", "cols"),
        P("month", "cols"),
        P("cols", None),
    )
    out_specs = P("month", "cols", None, None)
    return jax.shard_map(
        on_device, mesh=mesh, in_specs=in_specs, out_specs=out_specs, check_vma=False
    )
```

```python
import functools

import jax
import jax.numpy as jnp
from jax import lax
from jax.experimental import pallas as pl
from jax.experimental.pallas import tpu as pltpu
from jax.sharding import PartitionSpec as P

MESH = pl.DeviceIdType.MESH
CHUNKS = 4
HALVES = 2


def kernel(
    dims,
    cols_ref,
    count_ref,
    rows_ref,
    depth_ref,
    forcing_ref,
    tiles_ref,
    out_ref,
    tiles_v,
    x_rows,
    terms,
    pick,
    force_v,
    wet_v,
    back_v,
    send_v,
    recv_v,
    cols_v,
    cols_w,
    tile_sem,
    send_sem,
    recv_sem,
    back_send,
    back_recv,
    hand_send,
    hand_recv,
    table_send,
    table_recv,
    cols_sem,
):
    months, ncols, blk, tracers, block, slots = dims
    deltas = (0, ncols - 1, 1, ncols // 2)
    ngroups = len(deltas)
    everyone = tuple(range(ngroups))
    pad = x_rows.shape[1]
    part = tracers // HALVES
    per_chunk = slots // CHUNKS
    month = lax.axis_index("month")
    here = lax.axis_index("cols")
    last = months - 1
    odd = lax.rem(month, 2) == 1
    even = jnp.logical_not(odd)

    def tile_copy(k):
        rows = pl.ds(k * per_chunk, per_chunk)
        return pltpu.make_async_copy(tiles_ref.at[rows], tiles_v.at[0, rows], tile_sem.at[k])

    for k in range(CHUNKS):
        tile_copy(k).start()
    own_cols = pltpu.make_async_copy(cols_ref, cols_v.at[0], cols_sem)
    own_cols.start()

    barrier = pltpu.get_barrier_semaphore()

    def greet(other_month, groups):
        for g in groups:
            pl.semaphore_signal(
                barrier, inc=1,
                device_id={"month": other_month, "cols": lax.rem(here + deltas[g], ncols)},
                device_id_type=MESH,
            )

    @pl.when(odd)
    def _():
        greet(lax.rem(month + 2, months), everyone)
        greet(month, everyone[1:])
        greet(month - 1, (0,))

    @pl.when(month == last - 2)
    def _():
        greet(last - 1, everyone)

    @pl.when(month == last - 1)
    def _():
        greet(last, everyone)

    @pl.when(month == 0)
    def _():
        greet(1, everyone)

    @pl.when(even & (month > 0))
    def _():
        greet(month - 1, (0,))

    def meet():
        cases = (
            (month == 1, 3 * ngroups),
            (odd & (month > 1) & (month < last), 2 * ngroups),
            (month == last, 3 * ngroups - 1),
            (month == last - 1, ngroups + 1),
            (even & (month < last - 1), 1),
        )
        for case, peers in cases:
            @pl.when(case)
            def _():
                pl.semaphore_wait(barrier, peers)

    spread = (
        lax.broadcasted_iota(jnp.int32, (depth_ref.shape[1], block), 1) % depth_ref.shape[1]
        == lax.broadcasted_iota(jnp.int32, (depth_ref.shape[1], block), 0)
    ).astype(jnp.float32).astype(jnp.bfloat16)
    deep = jnp.dot(
        depth_ref[...].astype(jnp.float32).astype(jnp.bfloat16), spread,
        preferred_element_type=jnp.float32,
    )
    level = (lax.broadcasted_iota(jnp.int32, (blk, block), 1) // depth_ref.shape[1]).astype(jnp.float32)
    wet_v[...] = (level < deep).astype(jnp.float32)
    force_v[0] = forcing_ref[...]
    x_rows[...] = jnp.zeros_like(x_rows)
    live = lax.broadcasted_iota(jnp.int32, (blk, slots), 1) < count_ref[0, 0]
    inside = lax.broadcasted_iota(jnp.int32, (blk, slots), 0)
    for g, delta in enumerate(deltas):
        target = lax.rem(here + delta, ncols) * blk
        hit = ((inside + target) == rows_ref[...]) & live
        pick[0, g * blk:(g + 1) * blk, :] = hit.astype(jnp.float32).astype(jnp.bfloat16)
    own_cols.wait()

    def set_x(x):
        x = x.astype(jnp.bfloat16).astype(jnp.float32)
        for t in range(x.shape[0]):
            x_rows[0:blk, t, :] = x[t]

    def pair(g, held, swapped):
        s = 2 * g
        zero = jnp.zeros((pad, block), jnp.float32)
        xa = x_rows[cols_v[held, 0, s] & (blk - 1)]
        xb = x_rows[cols_v[held, 0, s + 1] & (blk - 1)]
        lhs = jnp.concatenate(
            [
                jnp.concatenate([xa, zero], 0).astype(jnp.bfloat16),
                jnp.concatenate([zero, xb], 0).astype(jnp.bfloat16),
            ], 1,
        )
        two = tiles_v[held, pl.ds(s, 2)]
        if swapped:
            out = jnp.dot(lhs, two.reshape(2 * block, block), preferred_element_type=jnp.float32)
        else:
            out = lax.dot_general(
                lhs, jnp.concatenate([two[0], two[1]], 1), (((1,), (1,)), ((), ())),
                preferred_element_type=jnp.float32,
            )
        terms[pl.ds(s * pad, 2 * pad), :] = out

    def link(turn, half, g, target_month, slot):
        if isinstance(g, int):
            shift = deltas[g]
        else:
            shift = jnp.where(g == 1, ncols - 1, 1)
        return pltpu.make_async_remote_copy(
            src_ref=send_v.at[turn, half, g],
            dst_ref=recv_v.at[slot, half, g],
            send_sem=send_sem.at[turn, half, g],
            recv_sem=recv_sem.at[slot, half, g],
            device_id={"month": target_month, "cols": lax.rem(here + shift, ncols)},
            device_id_type=MESH,
        )

    other = lax.rem(month + 2, months)
    far = jnp.where(lax.rem(here, 4) == 3, 2, 1)
    far_in = jnp.where(lax.rem(here, 4) == 0, 2, 1)

    def send_all(turn, half, target_month, slot, own):
        link(turn, half, far, target_month, slot).start()
        link(turn, half, 3, target_month, slot).start()
        link(turn, half, 3 - far, target_month, slot).start()
        if own is True:
            link(turn, half, 0, target_month, slot).start()
        else:
            @pl.when(own)
            def _():
                link(turn, half, 0, target_month, slot).start()

    def back(half):
        return pltpu.make_async_remote_copy(
            src_ref=back_v.at[half],
            dst_ref=out_ref.at[pl.ds(half * part, part)],
            send_sem=back_send.at[half],
            recv_sem=back_recv.at[half],
            device_id={"month": lax.rem(month + 1, months), "cols": here},
            device_id_type=MESH,
        )

    def hand(source, dest, send, recv):
        return pltpu.make_async_remote_copy(
            src_ref=source, dst_ref=dest, send_sem=send, recv_sem=recv,
            device_id={"month": lax.rem(month + 1, months), "cols": here},
            device_id_type=MESH,
        )

    def hand_tiles(k):
        rows = pl.ds(k * per_chunk, per_chunk)
        return hand(tiles_v.at[0, rows], tiles_v.at[1, rows], hand_send.at[k], hand_recv.at[k])

    def hand_tables():
        return (
            hand(pick.at[0], pick.at[1], table_send.at[0], table_recv.at[0]),
            hand(force_v.at[0], force_v.at[1], table_send.at[1], table_recv.at[1]),
            hand(cols_ref, cols_w, table_send.at[2], table_recv.at[2]),
        )

    def gather_rows(held, turn, half, first):
        columns = jnp.concatenate(
            [
                terms[pl.ds(first + t, slots, stride=pad), :].astype(jnp.bfloat16)
                for t in range(part)
            ], 1,
        )
        sums = jnp.dot(pick[held], columns, preferred_element_type=jnp.float32)
        sums = sums.astype(jnp.bfloat16)
        for t in range(part):
            for g in range(ngroups):
                send_v[turn, half, g, t] = sums[g * blk:(g + 1) * blk, t * block:(t + 1) * block]

    def total(slot, half):
        got = [recv_v[slot, half, g].astype(jnp.float32) for g in range(ngroups)]
        full = (got[0] + got[1]) + (got[2] + got[3])
        return full * wet_v[...][None]

    def turn_tiles(k):
        def one(i, carry):
            s = k * per_chunk + i
            tiles_v[0, s] = tiles_v[0, s].T
            return carry

        lax.fori_loop(0, per_chunk, one, 0, unroll=8)

    @pl.when(month == last)
    def _():
        set_x(force_v[0])
        for k in range(CHUNKS):
            tile_copy(k).wait()

            def run(i, carry):
                pair(k * (per_chunk // 2) + i, 0, False)
                return carry

            lax.fori_loop(0, per_chunk // 2, run, 0, unroll=per_chunk // 2)
        for half in range(HALVES):
            gather_rows(0, 0, half, half * part)
            if half == 0:
                meet()
            send_all(0, half, last - 1, 0, True)

        for k in range(CHUNKS):
            turn_tiles(k)

    @pl.when(month == last - 1)
    def _():
        for k in range(CHUNKS):
            tile_copy(k).wait()
            turn_tiles(k)
        meet()
        for copy in hand_tables():
            copy.start()

    @pl.when(even & (month < last - 1))
    def _():
        for k in range(CHUNKS):
            tile_copy(k).wait()
            turn_tiles(k)
            if k == 0:
                meet()
                for copy in hand_tables():
                    copy.start()
            hand_tiles(k).start()

    @pl.when(odd & (month < last))
    def _():
        for k in range(CHUNKS):
            tile_copy(k).wait()
            turn_tiles(k)
        meet()

    def step(turn, half):
        sweep = turn // 2
        held = lax.rem(turn, 2)
        opening = (month == last) & (sweep == 0)
        spare = (month == last - 1) & (turn == 0)
        took = jnp.where(month == last, 1, 0)
        ending = (month == 1) & (turn == 3)
        onward = jnp.where(ending, 0, lax.rem(month + months - 2, months))
        goes_to = jnp.where(spare, month - 1, jnp.where(held == 0, month, onward))
        wraps = jnp.where((month == 1) & (turn == 1), 2, 0)
        lands = jnp.where(ending, 0, 2 * sweep + wraps)
        lands_in = jnp.where(spare, 0, jnp.where(held == 0, turn + 1, lands))

        @pl.when(odd & (held == 1) & (half == 0) & (sweep == took))
        def _():
            for copy in hand_tables():
                copy.wait_recv()
            pair_cols = pltpu.make_async_copy(cols_w, cols_v.at[1], cols_sem)
            pair_cols.start()
            for c in range(CHUNKS):
                hand_tiles(c).wait_recv()
            pair_cols.wait()

        @pl.when((odd & jnp.logical_not(opening)) | spare)
        def _():
            @pl.when(held == 0)
            def _():
                link(turn, half, 0, other, turn).wait_recv()

            @pl.when(held == 1)
            def _():
                recv_v[turn, half, 0] = send_v[turn - held, half, 0]

            for g in (3, 3 - far_in):
                link(turn, half, g, other, turn).wait_recv()
            near = (
                recv_v[turn, half, 0].astype(jnp.float32)
                + recv_v[turn, half, 3 - far_in].astype(jnp.float32)
            ) + recv_v[turn, half, 3].astype(jnp.float32)
            push = force_v[held, pl.ds(half * part, part)]
            link(turn, half, far_in, other, turn).wait_recv()
            state = (near + recv_v[turn, half, far_in].astype(jnp.float32)) * wet_v[...][None]
            set_x(state + push)

            def run(i, carry):
                pair(i, held, True)
                return carry

            lax.fori_loop(0, slots // 2, run, 0, unroll=slots // 2)
            gather_rows(held, turn, half, 0)

            send_all(turn, half, goes_to, lands_in, (held == 1) | spare)

            @pl.when((sweep == 1) & (held == 1))
            def _():
                out_ref[pl.ds(half * part, part)] = total(turn, half)

            @pl.when((sweep == 1) & (held == 0) & (month < last))
            def _():
                back_v[half] = total(turn, half)
                back(half).start()

    def both(turn, carry):
        for half in range(HALVES):
            step(turn, half)
        return carry

    lax.fori_loop(0, 4, both, 0)

    @pl.when(month == last - 1)
    def _():
        for k in range(CHUNKS):
            hand_tiles(k).start()

    @pl.when(month == 0)
    def _():
        for half in range(HALVES):
            for g in range(ngroups):
                link(0, half, g, other, 0).wait_recv()
            out_ref[half * part:(half + 1) * part] = total(0, half)

    @pl.when(even)
    def _():
        for copy in hand_tables():
            copy.wait_send()
        for k in range(CHUNKS):
            hand_tiles(k).wait_send()

    @pl.when(even & (month > 0))
    def _():
        for half in range(HALVES):
            back(half).wait_recv()

    @pl.when((month == last - 1) | (month == last))
    def _():
        for half in range(HALVES):
            for g in range(ngroups):
                link(0, half, g, other, 0).wait_send()

    @pl.when(odd & (month < last))
    def _():
        for half in range(HALVES):
            back(half).wait_send()
            for g in range(1, ngroups):
                link(0, half, g, other, 0).wait_send()
            for g in range(ngroups):
                link(1, half, g, other, 0).wait_send()

    @pl.when(odd)
    def _():
        for half in range(HALVES):
            for g in range(1, ngroups):
                link(2, half, g, other, 0).wait_send()
            for g in range(ngroups):
                link(3, half, g, other, 0).wait_send()


def on_device(forcing, tiles, tile_rows, tile_cols, tile_count, depth):
    months = lax.axis_size("month")
    ncols = lax.axis_size("cols")
    _, blk, tracers, block = forcing.shape
    slots = tiles.shape[1]
    pad = 8
    part = tracers // HALVES
    dims = (months, ncols, blk, tracers, block, slots)
    vmem = pl.BlockSpec(memory_space=pltpu.VMEM)
    smem = pl.BlockSpec(memory_space=pltpu.SMEM)
    result = pl.pallas_call(
        functools.partial(kernel, dims),
        out_shape=pltpu.VMEM((tracers, blk, block), jnp.float32),
        in_specs=[vmem, smem, vmem, vmem, vmem, pl.BlockSpec(memory_space=pltpu.HBM)],
        out_specs=vmem,
        scratch_shapes=[
            pltpu.VMEM((2, slots, block, block), jnp.bfloat16),
            pltpu.VMEM((blk + 1, pad, block), jnp.float32),
            pltpu.VMEM((slots * pad + pad, block), jnp.float32),
            pltpu.VMEM((2, 4 * blk, slots), jnp.bfloat16),
            pltpu.VMEM((2, tracers, blk, block), jnp.float32),
            pltpu.VMEM((blk, block), jnp.float32),
            pltpu.VMEM((HALVES, part, blk, block), jnp.float32),
            pltpu.VMEM((4, HALVES, 4, part, blk, block), jnp.bfloat16),
            pltpu.VMEM((4, HALVES, 4, part, blk, block), jnp.bfloat16),
            pltpu.SMEM((2, 1, slots), jnp.int32),
            pltpu.VMEM((1, slots), jnp.int32),
            pltpu.SemaphoreType.DMA((CHUNKS,)),
            pltpu.SemaphoreType.DMA((4, HALVES, 4)),
            pltpu.SemaphoreType.DMA((4, HALVES, 4)),
            pltpu.SemaphoreType.DMA((HALVES,)),
            pltpu.SemaphoreType.DMA((HALVES,)),
            pltpu.SemaphoreType.DMA((CHUNKS,)),
            pltpu.SemaphoreType.DMA((CHUNKS,)),
            pltpu.SemaphoreType.DMA((3,)),
            pltpu.SemaphoreType.DMA((3,)),
            pltpu.SemaphoreType.DMA,
        ],
        compiler_params=pltpu.CompilerParams(
            collective_id=0, has_side_effects=True, vmem_limit_bytes=56 << 20
        ),
        name="year_sweeps",
    )(tile_cols, tile_count, tile_rows, depth, jnp.swapaxes(forcing[0], 0, 1), tiles[0])
    return jnp.swapaxes(result, 0, 1)[None]


def solution(mesh):
    in_specs = (
        P("month", "cols", None, None),
        P("month", "cols", None, None),
        P("month", "cols"),
        P("month", "cols"),
        P("month", "cols"),
        P("cols", None),
    )
    out_specs = P("month", "cols", None, None)
    return jax.shard_map(
        on_device, mesh=mesh, in_specs=in_specs, out_specs=out_specs, check_vma=False
    )
```
